256 devices in a mesh: blk: 32 (over y, z), row: 8 (over x, core).
Axes of the slice: x: 4, y: 4, z: 8, core: 2. Of those that a mesh axis runs over, the one named last changes fastest.
Arguments:
- far_kernel: bfloat16 [256, 8, 512, 512], P('blk', None, 'row'), may hold values from -0.25 to 0.25
- near_kernel: bfloat16 [256, 2, 512, 512], P('blk', None, 'row'), may hold values from -0.25 to 0.25
- samples: bfloat16 [256, 512, 128], P('blk'), may hold values from -18 to 18
- far_target: int32 [256, 8], P('blk'), may hold values from 0 to 255, as said below
Outputs:
- basis_out: float32 [256, 512, 128], P('blk', 'row')
- coupling: float32 [256, 8, 128, 128], P('blk', None, 'row')
- parent_samples: float32 [128, 256, 128], P('blk', 'row')
The draws below stay inside these ranges and needn't reach their ends.
Inputs may be any that keep to these rules, and one draw needn't show every extreme that they name: `far_target`: each row names 8 different target clusters; among the far blocks of the source clusters of one index of blk (rows 8 * g to 8 * g + 7), at most 4 name targets of any one index of blk (clusters 8 * h to 8 * h + 7), and exactly 4 for some such index.
All inputs are finite; a program needn't handle non-finite values.
Results may differ from the reference program's by a relative error of at most 0.02.
Values may be sent and summed in bfloat16 or wider, within the bound.
No kernel may reach another device: no remote copies, remote signals or barrier semaphores. Data moves between devices by JAX's collectives and lax.ppermute only.
A program may use at most 64 MiB of HBM per device.

```python
import math
import jax
import jax.numpy as jnp
from jax import lax

R = 512
S = 128
F = 8
ITERS = 12
CL_G = 8
C = 256
CAP = 4


def draw_samples(key, part):
    key_cols = jax.random.fold_in(key, 0)
    key_vals = jax.random.fold_in(key, 2)
    col_scale = jnp.exp(jax.random.uniform(key_cols, (S,), jnp.float32, math.log(0.02), 0.0))
    values = jnp.clip(jax.random.normal(key_vals, (C, R, S), jnp.float32), -6.0, 6.0)
    return (values * col_scale[None, None, :]).astype(jnp.bfloat16)


def draw_far_target(key, part):
    group_total = C // CL_G
    slot_total = CL_G * F

    def one_group(group_key):
        key_full, key_pool, key_order, key_offset = jax.random.split(group_key, 4)
        full_group = jax.random.randint(key_full, (), 0, group_total).astype(jnp.int32)
        pool = jnp.tile(jnp.arange(group_total, dtype=jnp.int32), CAP)
        scores = jax.random.permutation(key_pool, group_total * CAP).astype(jnp.int32)
        scores = jnp.where(pool == full_group, scores - group_total * CAP, scores)
        ordered = pool[jnp.argsort(scores, stable=True)][:slot_total]
        chosen = ordered[jax.random.permutation(key_order, slot_total)]
        hits = (chosen[:, None] == jnp.arange(group_total, dtype=jnp.int32)[None, :]).astype(jnp.int32)
        rank = jnp.sum((jnp.cumsum(hits, axis=0) - 1) * hits, axis=1)
        offset = jax.random.randint(key_offset, (group_total,), 0, CL_G).astype(jnp.int32)
        local = (offset[chosen] + rank) % CL_G
        return (chosen * CL_G + local).reshape(CL_G, F)
    keys = jax.random.split(key, group_total)
    return jax.vmap(one_group)(keys).reshape(C, F).astype(jnp.int32)


def block_levels(stream_key, shape, cuts, smallest, largest):
    loudness = 1.0
    for dim, parts in cuts:
        steps = jax.random.uniform(jax.random.fold_in(jax.random.fold_in(stream_key, 6), dim), (parts,), jnp.float32, smallest / len(cuts), largest / len(cuts))
        loudness = loudness * jnp.repeat(jnp.exp(steps), shape[dim] // parts).reshape((-1,) + (1,) * (len(shape) - 1 - dim))
    return loudness


def scatter_about(key, shape, deviation, reach, cuts=(), held_as=jnp.bfloat16):
    values = deviation * jax.random.normal(key, shape, jnp.float32)
    if cuts:
        values = values * block_levels(key, shape, cuts, -0.22, 0.18)
    return jnp.clip(values, -reach, reach).astype(held_as)


def setup_inputs(seed: int = 0) -> dict:
    splits = jax.random.split(jax.random.key(seed), 5)
    far_kernel = scatter_about(splits[0], (C, F, R, R), R ** -0.5, 0.25, ((0, 32), (2, 8)))
    near_kernel = scatter_about(splits[1], (C, 2, R, R), R ** -0.5, 0.25, ((0, 32), (2, 8)))
    samples = draw_samples(jax.random.fold_in(splits[4], 71), 0)
    far_target = draw_far_target(jax.random.fold_in(splits[4], 71), 0)
    return {"far_kernel": far_kernel, "near_kernel": near_kernel, "samples": samples, "far_target": far_target}


def reference(far_kernel, near_kernel, samples, far_target):
    highest = lax.Precision.HIGHEST

    def far_apply(operands):
        blocks, sample = operands
        flat = blocks.reshape(F * R, R)
        result = jnp.dot(flat, sample, preferred_element_type=jnp.float32)
        return result.reshape(F, R, S).astype(jnp.bfloat16)
    far_product = lax.map(far_apply, (far_kernel, samples))
    far_sketch = jax.ops.segment_sum(far_product.astype(jnp.float32).reshape(C * F, R, S), far_target.reshape(C * F).astype(jnp.int32), num_segments=C)
    sibling = samples.reshape(C // 2, 2, R, S)[:, ::-1].reshape(C, R, S)

    def near_apply(operands):
        blocks, own_rows, other_rows = operands
        joined = jnp.concatenate([blocks[0], blocks[1]], axis=1)
        stacked = jnp.concatenate([own_rows, other_rows], axis=0)
        return jnp.dot(joined, stacked, preferred_element_type=jnp.float32)
    near_sum = lax.map(near_apply, (near_kernel, samples, sibling))
    sketch = far_sketch - near_sum
    gram_mat = jnp.einsum('crs,crt->cst', sketch, sketch, precision=highest)
    mean_sq = jnp.trace(gram_mat, axis1=1, axis2=2) / (R * S) + 1e-06
    identity = jnp.eye(S, dtype=jnp.float32)
    level_mat = gram_mat / (R * S * mean_sq)[:, None, None]
    root_mat = jnp.broadcast_to(identity, gram_mat.shape)
    for sweep_index in range(ITERS):
        step_mat = 1.5 * identity - 0.5 * jnp.matmul(root_mat, level_mat, precision=highest)
        level_mat = jnp.matmul(level_mat, step_mat, precision=highest)
        root_mat = jnp.matmul(step_mat, root_mat, precision=highest)
    basis_out = jnp.einsum('crs,cst->crt', sketch, root_mat, precision=highest) / jnp.sqrt(S * mean_sq)[:, None, None]
    basis_half = basis_out.astype(jnp.bfloat16)
    mixed_rows = lax.map(far_apply, (far_kernel, basis_half))

    def couple(operands):
        mixed_one, target_row = operands
        picked = jnp.take(basis_half, target_row, axis=0)
        return jnp.einsum('frs,frt->fst', picked.astype(jnp.float32), mixed_one.astype(jnp.float32))
    coupling = lax.map(couple, (mixed_rows, far_target)) / jnp.sqrt(jnp.float32(R))
    projected = jnp.einsum('crs,crt->cst', basis_half.astype(jnp.float32), samples.astype(jnp.float32)) / jnp.sqrt(jnp.float32(R))
    parent_samples = projected.reshape(C // 2, 2 * S, S)
    return (basis_out, coupling, parent_samples)
```

```python
import functools

import jax
import jax.numpy as jnp
from jax import lax
from jax.experimental import pallas as pl
from jax.experimental.pallas import tpu as pltpu
from jax.sharding import Mesh, PartitionSpec as P

ITERS = 12
SLOTS = 4
META = 8
BF16 = jnp.bfloat16
F32 = jnp.float32
SMEM_SPEC = pl.BlockSpec(memory_space=pltpu.SMEM)
BLK = ("y", "z")
ROW = ("x", "core")


def whole(shape):
    return pl.BlockSpec(shape, lambda *_: (0,) * len(shape))


def far_kernel_body(groups, target, far, near, own, sibling, send, minus_near, slot_of, count, slot_id):
    j = pl.program_id(0)
    far_count, rows, width = far.shape[1:]
    local = target.shape[0]

    @pl.when(j == 0)
    def _():
        def clear_count(i, carry):
            count[i] = 0
            return carry

        def clear_id(i, carry):
            slot_id[i] = -1
            return carry

        lax.fori_loop(0, groups, clear_count, 0)
        lax.fori_loop(0, groups * SLOTS, clear_id, 0)

        def place(b, carry):
            t = target[b // far_count, b % far_count]
            h = jnp.clip(t // local, 0, groups - 1)
            c = jnp.minimum(count[h], SLOTS - 1)
            count[h] = c + 1
            slot_of[b] = h * SLOTS + c
            slot_id[h * SLOTS + c] = t % local
            return carry

        lax.fori_loop(0, local * far_count, place, 0)
        row = lax.broadcasted_iota(jnp.int32, (META, send.shape[2]), 0)

        def header(h, carry):
            send[h, : SLOTS * rows] = jnp.zeros((SLOTS * rows, send.shape[2]), BF16)
            ids = jnp.full(row.shape, -1, jnp.int32)
            for c in range(SLOTS):
                ids = jnp.where(row == c, slot_id[h * SLOTS + c], ids)
            send[h, SLOTS * rows :] = ids.astype(F32).astype(BF16)
            return carry

        lax.fori_loop(0, groups, header, 0)

    product = jnp.dot(far[0].reshape(far_count * rows, width), own[0], preferred_element_type=F32)
    product = product.astype(BF16).reshape(far_count, rows, send.shape[2])
    for k in range(far_count):
        q = slot_of[j * far_count + k]
        start = pl.multiple_of((q % SLOTS) * rows, rows)
        send[q // SLOTS, pl.ds(start, rows)] = product[k]
    near_sum = jnp.dot(near[0, 0], own[0], preferred_element_type=F32)
    near_sum += jnp.dot(near[0, 1], sibling[0], preferred_element_type=F32)
    minus_near[0] = -near_sum


def far_products(far_kernel, near_kernel, samples, far_target, groups):
    local, far_count, rows, width = far_kernel.shape
    cols = samples.shape[2]
    depth = SLOTS * rows + META
    flops = 2 * local * (far_count + 2) * rows * width * cols
    return pl.pallas_call(
        functools.partial(far_kernel_body, groups),
        grid=(local,),
        in_specs=[
            SMEM_SPEC,
            pl.BlockSpec((1, far_count, rows, width), lambda j: (j, 0, 0, 0)),
            pl.BlockSpec((1, 2, rows, width), lambda j: (j, 0, 0, 0)),
            pl.BlockSpec((1, width, cols), lambda j: (j, 0, 0)),
            pl.BlockSpec((1, width, cols), lambda j: (j + 1 - 2 * (j % 2), 0, 0)),
        ],
        out_specs=[
            whole((groups, depth, cols)),
            pl.BlockSpec((1, rows, cols), lambda j: (j, 0, 0)),
            SMEM_SPEC,
        ],
        out_shape=[
            jax.ShapeDtypeStruct((groups, depth, cols), BF16),
            jax.ShapeDtypeStruct((local, rows, cols), F32),
            jax.ShapeDtypeStruct((local * far_count,), jnp.int32),
        ],
        scratch_shapes=[pltpu.SMEM((groups,), jnp.int32), pltpu.SMEM((groups * SLOTS,), jnp.int32)],
        cost_estimate=pl.CostEstimate(flops=flops, bytes_accessed=9000000, transcendentals=0),
        name="far_products",
    )(far_target, far_kernel, near_kernel, samples, samples)


def gather_sum_body(ids, received, minus_near, sketch, *partial):
    local, rows, cols = minus_near.shape
    for acc in partial:
        acc[...] = jnp.zeros_like(acc)

    def step(g, carry):
        for c in range(SLOTS):
            at = ids[g, c]
            at = jnp.where((at < 0) | (at >= local), local, at)
            partial[c][at] = partial[c][at] + received[g, c * rows : (c + 1) * rows].astype(F32)
        return carry

    lax.fori_loop(0, received.shape[0], step, 0)
    total = minus_near[...]
    for acc in partial:
        total = total + acc[:local]
    sketch[...] = total


def gather_sum(ids, received, minus_near):
    local, rows, cols = minus_near.shape
    return pl.pallas_call(
        gather_sum_body,
        in_specs=[SMEM_SPEC, whole(received.shape), whole(minus_near.shape)],
        out_specs=whole(minus_near.shape),
        grid=(1,),
        out_shape=jax.ShapeDtypeStruct(minus_near.shape, F32),
        scratch_shapes=[pltpu.VMEM((local + 1, rows, cols), F32)] * SLOTS,
        cost_estimate=pl.CostEstimate(flops=2000000, bytes_accessed=3000000, transcendentals=0),
        name="gather_sum",
    )(ids, received, minus_near)


def basis_body(sketch, basis, basis_half):
    highest = lax.Precision.HIGHEST
    full_width, cols = sketch.shape
    dot = functools.partial(jnp.dot, precision=highest, preferred_element_type=F32)
    values = sketch[...]
    gram = lax.dot_general(
        values, values, (((0,), (0,)), ((), ())), precision=highest, preferred_element_type=F32
    )
    identity = (
        lax.broadcasted_iota(jnp.int32, (cols, cols), 0) == lax.broadcasted_iota(jnp.int32, (cols, cols), 1)
    ).astype(F32)
    trace = jnp.sum(jnp.sum(gram * identity, axis=1, keepdims=True), axis=0, keepdims=True)
    mean_sq = trace / (full_width * cols) + 1e-6
    level = gram / (full_width * cols * mean_sq)
    root = 1.5 * identity - 0.5 * level
    level = dot(level, root)
    for _ in range(ITERS - 2):
        step = 1.5 * identity - 0.5 * dot(root, level)
        level = dot(level, step)
        root = dot(step, root)
    step = 1.5 * identity - 0.5 * dot(root, level)
    root = dot(step, root)
    result = dot(values, root / jnp.sqrt(cols * mean_sq))
    basis[...] = result
    basis_half[...] = result.astype(BF16)


def basis_of(sketch):
    return pl.pallas_call(
        basis_body,
        in_specs=[whole(sketch.shape)],
        out_specs=[whole(sketch.shape)] * 2,
        grid=(1,),
        out_shape=[jax.ShapeDtypeStruct(sketch.shape, F32), jax.ShapeDtypeStruct(sketch.shape, BF16)],
        cost_estimate=pl.CostEstimate(flops=2000000000, bytes_accessed=1000000, transcendentals=0),
        name="basis_of",
    )(sketch)


def pick_body(ids, basis, send, half):
    local, rows, cols = basis.shape
    half[:local] = basis[...].astype(BF16)
    half[local] = jnp.zeros((rows, cols), BF16)

    def step(g, carry):
        for c in range(SLOTS):
            at = ids[g, c]
            at = jnp.where((at < 0) | (at >= local), local, at)
            send[g, c * rows : (c + 1) * rows] = half[at]
        return carry

    lax.fori_loop(0, send.shape[0], step, 0)


def pick(ids, basis):
    local, rows, cols = basis.shape
    groups = ids.shape[0]
    shape = (groups, SLOTS * rows, cols)
    return pl.pallas_call(
        pick_body,
        in_specs=[SMEM_SPEC, whole(basis.shape)],
        out_specs=whole(shape),
        grid=(1,),
        out_shape=jax.ShapeDtypeStruct(shape, BF16),
        scratch_shapes=[pltpu.VMEM((local + 1, rows, cols), BF16)],
        cost_estimate=pl.CostEstimate(flops=1000000, bytes_accessed=3000000, transcendentals=0),
        name="pick",
    )(ids, basis)


def coupling_body(slot_of, place, far, segment, picked, samples, mine, other, parent, scratch):
    j = pl.program_id(0)
    far_count, rows, width = far.shape[1:]
    cols = segment.shape[2]
    x_count, _, out_rows, _ = mine.shape
    core = place[1]
    mixed = jnp.dot(far[0].reshape(far_count * rows, width), segment[0], preferred_element_type=F32)
    mixed = mixed.astype(BF16).reshape(far_count, rows, cols)
    for k in range(far_count):
        q = slot_of[j * far_count + k]
        start = pl.multiple_of((q % SLOTS) * rows, rows)
        basis_rows = picked[q // SLOTS, pl.ds(start, rows)]
        part = lax.dot_general(
            basis_rows, mixed[k], (((0,), (0,)), ((), ())), preferred_element_type=F32
        )
        part = part.reshape(x_count, 2, out_rows, cols)
        mine[:, k] = jnp.where(core == 0, part[:, 0], part[:, 1]).astype(BF16)
        other[:, k] = jnp.where(core == 0, part[:, 1], part[:, 0]).astype(BF16)
    place_in_pair = place[0] // 4

    @pl.when(j % 2 == place_in_pair)
    def _():
        scratch[...] = lax.dot_general(
            segment[0], samples[0], (((0,), (0,)), ((), ())), preferred_element_type=F32
        ) / jnp.sqrt(F32(width))
        count = parent.shape[1]
        start = pl.multiple_of((place[0] % 4) * count, count)
        parent[j // 2] = scratch[pl.ds(start, count)]


def coupling_parts(slot_of, place, far_kernel, segment, picked, samples, x_count):
    local, far_count, rows, width = far_kernel.shape
    cols = segment.shape[2]
    blocks = local * far_count
    out_rows = cols // (2 * x_count)
    parent_rows = 2 * cols // (2 * x_count)
    flops = 2 * blocks * rows * cols * (width + cols)
    part_spec = pl.BlockSpec((x_count, far_count, out_rows, cols), lambda j: (0, j, 0, 0))
    part_shape = jax.ShapeDtypeStruct((x_count, blocks, out_rows, cols), BF16)
    return pl.pallas_call(
        coupling_body,
        grid=(local,),
        in_specs=[
            SMEM_SPEC,
            SMEM_SPEC,
            pl.BlockSpec((1, far_count, rows, width), lambda j: (j, 0, 0, 0)),
            pl.BlockSpec((1, width, cols), lambda j: (j, 0, 0)),
            whole(picked.shape),
            pl.BlockSpec((1, width, cols), lambda j: (j, 0, 0)),
        ],
        out_specs=[part_spec, part_spec, whole((local // 2, parent_rows, cols))],
        out_shape=[part_shape, part_shape, jax.ShapeDtypeStruct((local // 2, parent_rows, cols), F32)],
        scratch_shapes=[pltpu.VMEM((cols, cols), F32)],
        cost_estimate=pl.CostEstimate(flops=flops, bytes_accessed=10000000, transcendentals=0),
        name="coupling_parts",
    )(slot_of, place, far_kernel, segment, picked, samples)


def per_device(far_kernel, near_kernel, samples, far_target):
    local, far_count, rows, width = far_kernel.shape
    cols = samples.shape[2]
    groups = lax.axis_size("y") * lax.axis_size("z")
    x_count = lax.axis_size("x")
    core = lax.axis_index("core")
    place = jnp.stack([lax.axis_index("x") * 2 + core, core]).astype(jnp.int32)

    send, minus_near, slot_of = far_products(far_kernel, near_kernel, samples, far_target, groups)
    received = lax.all_to_all(send, BLK, 0, 0, tiled=True)
    ids = received[:, SLOTS * rows :, 0].astype(jnp.int32)
    sketch = gather_sum(ids, received, minus_near)
    sketch = lax.all_to_all(sketch, ROW, 0, 0, tiled=True)
    basis, basis_half = basis_of(sketch.reshape(width, cols))
    basis_out = lax.all_to_all(basis.reshape(local, rows, cols), ROW, 0, 0, tiled=True)
    segment = lax.all_gather(basis_half, ROW, axis=0, tiled=True).reshape(local, width, cols)
    picked = lax.all_to_all(pick(ids, basis_out), BLK, 0, 0, tiled=True)
    mine, other, parent = coupling_parts(
        slot_of, place, far_kernel, segment, picked, samples, x_count
    )
    partner = lax.ppermute(other, "core", [(0, 1), (1, 0)])
    pair = (mine.astype(F32) + partner.astype(F32)).astype(BF16)
    parts = lax.all_to_all(pair, "x", 0, 0, tiled=True)
    coupling = jnp.sum(parts.astype(F32), axis=0) / jnp.sqrt(F32(width))
    return basis_out, coupling.reshape(local, far_count, cols // (2 * x_count), cols), parent


def solution(mesh):
    fine = Mesh(mesh.devices.reshape(4, 8, 4, 2), ("y", "z", "x", "core"))
    return jax.shard_map(
        per_device,
        mesh=fine,
        in_specs=(
            P(BLK, None, ROW, None),
            P(BLK, None, ROW, None),
            P(BLK, None, None),
            P(BLK, None),
        ),
        out_specs=(P(BLK, ROW, None), P(BLK, None, ROW, None), P(BLK, ROW, None)),
        check_vma=False,
    )
```

```python
import functools

import jax
import jax.numpy as jnp
from jax import lax
from jax.experimental import pallas as pl
from jax.experimental.pallas import tpu as pltpu
from jax.sharding import Mesh, PartitionSpec as P

ITERS = 12
SLOTS = 4
META = 8
BF16 = jnp.bfloat16
F32 = jnp.float32
SMEM_SPEC = pl.BlockSpec(memory_space=pltpu.SMEM)
VMEM_SPEC = pl.BlockSpec(memory_space=pltpu.VMEM)
BLK = ("y", "z")
ROW = ("x", "core")


def whole(shape):
    return pl.BlockSpec(shape, lambda *_: (0,) * len(shape))


def far_kernel_body(groups, target, far, samples, send, slot_of, count, slot_id):
    step = pl.program_id(0)
    pair, far_count, rows, width = far.shape
    cols = send.shape[2]
    local = target.shape[0]

    @pl.when(step == 0)
    def _():
        for i in range(groups):
            count[i] = 0
        for i in range(groups * SLOTS):
            slot_id[i] = -1

        def clear(h, carry):
            send[h, : SLOTS * rows] = jnp.zeros((SLOTS * rows, cols), BF16)
            return carry

        lax.fori_loop(0, groups, clear, 0)

    for i in range(pair):
        j = step * pair + i
        product = jnp.dot(far[i].reshape(far_count * rows, width), samples[i], preferred_element_type=F32)
        product = product.astype(BF16).reshape(far_count, rows, cols)
        for k in range(far_count):
            t = target[j, k]
            h = jnp.clip(t // local, 0, groups - 1)
            c = jnp.minimum(count[h], SLOTS - 1)
            count[h] = c + 1
            slot_of[j * far_count + k] = h * SLOTS + c
            slot_id[h * SLOTS + c] = t % local
            start = pl.multiple_of(c * rows, rows)
            send[h, pl.ds(start, rows)] = product[k]

    @pl.when(step == pl.num_programs(0) - 1)
    def _():
        row = lax.broadcasted_iota(jnp.int32, (META, cols), 0)

        def header(h, carry):
            ids = jnp.full(row.shape, -1, jnp.int32)
            for c in range(SLOTS):
                ids = jnp.where(row == c, slot_id[h * SLOTS + c], ids)
            send[h, SLOTS * rows :] = ids.astype(F32).astype(BF16)
            return carry

        lax.fori_loop(0, groups, header, 0, unroll=4)


def far_products(far_kernel, samples, far_target, groups):
    local, far_count, rows, width = far_kernel.shape
    cols = samples.shape[2]
    depth = SLOTS * rows + META
    pair = 2
    flops = 2 * local * far_count * rows * width * cols
    return pl.pallas_call(
        functools.partial(far_kernel_body, groups),
        grid=(local // pair,),
        in_specs=[
            SMEM_SPEC,
            pl.BlockSpec((pair, far_count, rows, width), lambda j: (j, 0, 0, 0)),
            pl.BlockSpec((pair, width, cols), lambda j: (j, 0, 0)),
        ],
        out_specs=[VMEM_SPEC, SMEM_SPEC],
        out_shape=[
            jax.ShapeDtypeStruct((groups, depth, cols), BF16),
            jax.ShapeDtypeStruct((local * far_count,), jnp.int32),
        ],
        scratch_shapes=[pltpu.SMEM((groups,), jnp.int32), pltpu.SMEM((groups * SLOTS,), jnp.int32)],
        cost_estimate=pl.CostEstimate(flops=flops, bytes_accessed=7500000, transcendentals=0),
        name="far_products",
    )(far_target, far_kernel, samples)


def near_body(near, samples, minus_near):
    for i in range(2):
        near_sum = jnp.dot(near[i, 0], samples[i], preferred_element_type=F32)
        near_sum += jnp.dot(near[i, 1], samples[1 - i], preferred_element_type=F32)
        minus_near[i] = -near_sum


def near_products(near_kernel, samples):
    local, _, rows, width = near_kernel.shape
    cols = samples.shape[2]
    return pl.pallas_call(
        near_body,
        grid=(local // 2,),
        in_specs=[
            pl.BlockSpec((2, 2, rows, width), lambda j: (j, 0, 0, 0)),
            pl.BlockSpec((2, width, cols), lambda j: (j, 0, 0)),
        ],
        out_specs=pl.BlockSpec((2, rows, cols), lambda j: (j, 0, 0)),
        out_shape=jax.ShapeDtypeStruct((local, rows, cols), F32),
        cost_estimate=pl.CostEstimate(
            flops=4 * local * rows * width * cols, bytes_accessed=2500000, transcendentals=0
        ),
        name="near_products",
    )(near_kernel, samples)


def gather_sum_body(ids, received, minus_near, sketch, *partial):
    local, rows, cols = minus_near.shape
    for acc in partial:
        acc[...] = jnp.zeros_like(acc)

    def step(g, carry):
        for c in range(SLOTS):
            at = ids[g, c]
            at = jnp.where((at < 0) | (at >= local), local, at)
            partial[c][at] = partial[c][at] + received[g, c * rows : (c + 1) * rows].astype(F32)
        return carry

    lax.fori_loop(0, received.shape[0], step, 0)
    total = minus_near[...]
    for acc in partial:
        total = total + acc[:local]
    sketch[...] = total.astype(BF16)


def gather_sum(ids, received, minus_near):
    local, rows, cols = minus_near.shape
    return pl.pallas_call(
        gather_sum_body,
        in_specs=[SMEM_SPEC, VMEM_SPEC, VMEM_SPEC],
        out_specs=VMEM_SPEC,
        out_shape=jax.ShapeDtypeStruct(minus_near.shape, BF16),
        scratch_shapes=[pltpu.VMEM((local + 1, rows, cols), F32)] * SLOTS,
        cost_estimate=pl.CostEstimate(flops=2000000, bytes_accessed=3000000, transcendentals=0),
        name="gather_sum",
    )(ids, received, minus_near)


def basis_body(sketch, basis_half):
    highest = lax.Precision.HIGHEST
    full_width, cols = sketch.shape
    dot = functools.partial(jnp.dot, precision=highest, preferred_element_type=F32)
    values = sketch[...].astype(F32)
    gram = lax.dot_general(
        values, values, (((0,), (0,)), ((), ())), precision=highest, preferred_element_type=F32
    )
    identity = (
        lax.broadcasted_iota(jnp.int32, (cols, cols), 0) == lax.broadcasted_iota(jnp.int32, (cols, cols), 1)
    ).astype(F32)
    trace = jnp.sum(jnp.sum(gram * identity, axis=1, keepdims=True), axis=0, keepdims=True)
    mean_sq = trace / (full_width * cols) + 1e-6
    level = gram / (full_width * cols * mean_sq)
    root = 1.5 * identity - 0.5 * level
    level = dot(level, root)
    for _ in range(ITERS - 2):
        step = 1.5 * identity - 0.5 * dot(root, level)
        level = dot(level, step)
        root = dot(step, root)
    step = 1.5 * identity - 0.5 * dot(root, level)
    root = dot(step, root)
    result = dot(values, root / jnp.sqrt(cols * mean_sq))
    basis_half[...] = result.astype(BF16)


def basis_of(sketch):
    return pl.pallas_call(
        basis_body,
        in_specs=[VMEM_SPEC],
        out_specs=VMEM_SPEC,
        out_shape=jax.ShapeDtypeStruct(sketch.shape, BF16),
        cost_estimate=pl.CostEstimate(flops=2000000000, bytes_accessed=1000000, transcendentals=0),
        name="basis_of",
    )(sketch)


def pick_body(ids, basis, send, basis_out):
    local, rows, _ = basis.shape

    def step(g, carry):
        for c in range(SLOTS):
            at = jnp.clip(ids[g, c], 0, local - 1)
            send[g, c * rows : (c + 1) * rows] = basis[at]
        return carry

    lax.fori_loop(0, send.shape[0], step, 0, unroll=2)
    basis_out[...] = basis[...].astype(F32)


def pick(ids, basis):
    local, rows, cols = basis.shape
    groups = ids.shape[0]
    shape = (groups, SLOTS * rows, cols)
    return pl.pallas_call(
        pick_body,
        in_specs=[SMEM_SPEC, VMEM_SPEC],
        out_specs=[VMEM_SPEC, VMEM_SPEC],
        out_shape=[jax.ShapeDtypeStruct(shape, BF16), jax.ShapeDtypeStruct(basis.shape, F32)],
        cost_estimate=pl.CostEstimate(flops=1000000, bytes_accessed=3000000, transcendentals=0),
        name="pick",
    )(ids, basis)


def coupling_body(slot_of, place, far, own, across, picked, samples, mine, other, parent, scratch):
    j = pl.program_id(0)
    far_count, rows, width = far.shape[1:]
    cols = own.shape[2]
    x_count, _, out_rows, _ = mine.shape
    core = place[1]
    segment = jnp.where(j % 2 == core, own[0], across[0])
    mixed = jnp.dot(far[0].reshape(far_count * rows, width), segment, preferred_element_type=F32)
    mixed = mixed.astype(BF16).reshape(far_count, rows, cols)
    zero = jnp.zeros((rows, cols), BF16)
    for k in range(0, far_count, 2):
        basis_rows = []
        for i in range(2):
            q = slot_of[j * far_count + k + i]
            start = pl.multiple_of((q % SLOTS) * rows, rows)
            basis_rows.append(picked[q // SLOTS, pl.ds(start, rows)])
        right = jnp.concatenate(
            [
                jnp.concatenate([mixed[k], zero], axis=1),
                jnp.concatenate([zero, mixed[k + 1]], axis=1),
            ],
            axis=0,
        )
        both = lax.dot_general(
            jnp.concatenate(basis_rows, axis=0),
            right,
            (((0,), (0,)), ((), ())),
            preferred_element_type=F32,
        )
        for i in range(2):
            part = both[:, i * cols : (i + 1) * cols].reshape(x_count, 2, out_rows, cols)
            mine[:, k + i] = jnp.where(core == 0, part[:, 0], part[:, 1]).astype(BF16)
            other[:, k + i] = jnp.where(core == 0, part[:, 1], part[:, 0]).astype(BF16)

    @pl.when(j % 2 == place[0] // 4)
    def _():
        scratch[...] = lax.dot_general(
            segment, samples[0], (((0,), (0,)), ((), ())), preferred_element_type=F32
        ) / jnp.sqrt(F32(width))
        count = parent.shape[1]
        start = pl.multiple_of((place[0] % 4) * count, count)
        parent[j // 2] = scratch[pl.ds(start, count)]


def coupling_parts(slot_of, place, far_kernel, own, across, picked, samples):
    local, far_count, rows, width = far_kernel.shape
    x_count, _, cols = own.shape
    blocks = local * far_count
    out_rows = cols // local
    parent_rows = 2 * cols // local
    flops = 2 * blocks * rows * cols * (width + cols)
    part_spec = pl.BlockSpec((x_count, far_count, out_rows, cols), lambda j, *_: (0, j, 0, 0))
    part_shape = jax.ShapeDtypeStruct((x_count, blocks, out_rows, cols), BF16)
    side = pl.BlockSpec(
        (1, width, cols), lambda j, slots, place: ((place[0] // 2 + x_count - j // 2) % x_count, 0, 0)
    )
    return pl.pallas_call(
        coupling_body,
        grid_spec=pltpu.PrefetchScalarGridSpec(
            num_scalar_prefetch=2,
            grid=(local,),
            in_specs=[
                pl.BlockSpec((1, far_count, rows, width), lambda j, *_: (j, 0, 0, 0)),
                side,
                side,
                VMEM_SPEC,
                pl.BlockSpec((1, width, cols), lambda j, *_: (j, 0, 0)),
            ],
            out_specs=[part_spec, part_spec, VMEM_SPEC],
            scratch_shapes=[pltpu.VMEM((cols, cols), F32)],
        ),
        out_shape=[part_shape, part_shape, jax.ShapeDtypeStruct((local // 2, parent_rows, cols), F32)],
        cost_estimate=pl.CostEstimate(flops=flops, bytes_accessed=10000000, transcendentals=0),
        name="coupling_parts",
    )(slot_of, place, far_kernel, own, across, picked, samples)


def per_device(far_kernel, near_kernel, samples, far_target):
    local, far_count, rows, width = far_kernel.shape
    cols = samples.shape[2]
    groups = lax.axis_size("y") * lax.axis_size("z")
    x_count = lax.axis_size("x")
    core = lax.axis_index("core")
    place = jnp.stack([lax.axis_index("x") * 2 + core, core]).astype(jnp.int32)

    send, slot_of = far_products(far_kernel, samples, far_target, groups)
    received = lax.all_to_all(send, BLK, 0, 0, tiled=True)
    minus_near = near_products(near_kernel, samples)
    ids = received[:, SLOTS * rows :, 0].astype(jnp.int32)
    received = pltpu.with_memory_space_constraint(received, pltpu.VMEM)
    sketch = gather_sum(ids, received, minus_near)
    sketch = lax.all_to_all(sketch, ROW, 0, 0, tiled=True)
    basis = basis_of(sketch.reshape(width, cols))
    basis_rows = lax.all_to_all(basis.reshape(local, rows, cols), ROW, 0, 0, tiled=True)
    send_rows, basis_out = pick(ids, basis_rows)
    picked = lax.all_to_all(send_rows, BLK, 0, 0, tiled=True)
    picked = pltpu.with_memory_space_constraint(picked, pltpu.VMEM)
    shifted = [
        lax.ppermute(basis, "x", [(i, (i + d) % x_count) for i in range(x_count)]) for d in range(1, x_count)
    ]
    own = jnp.stack([basis] + shifted)
    across = lax.ppermute(own, "core", [(0, 1), (1, 0)])
    mine, other, parent = coupling_parts(slot_of, place, far_kernel, own, across, picked, samples)
    partner = lax.ppermute(other, "core", [(0, 1), (1, 0)])
    pair = (mine.astype(F32) + partner.astype(F32)).astype(BF16)
    parts = lax.all_to_all(pair, "x", 0, 0, tiled=True)
    coupling = jnp.sum(parts.astype(F32), axis=0) / jnp.sqrt(F32(width))
    return basis_out, coupling.reshape(local, far_count, cols // (2 * x_count), cols), parent


def solution(mesh):
    fine = Mesh(mesh.devices.reshape(4, 8, 4, 2), ("y", "z", "x", "core"))
    return jax.shard_map(
        per_device,
        mesh=fine,
        in_specs=(
            P(BLK, None, ROW, None),
            P(BLK, None, ROW, None),
            P(BLK, None, None),
            P(BLK, None),
        ),
        out_specs=(P(BLK, ROW, None), P(BLK, None, ROW, None), P(BLK, ROW, None)),
        check_vma=False,
    )
```

```python
import functools

import jax
import jax.numpy as jnp
from jax import lax
from jax.experimental import pallas as pl
from jax.experimental.pallas import tpu as pltpu
from jax.sharding import Mesh, PartitionSpec as P

ITERS = 12
SLOTS = 4
META = 8
BF16 = jnp.bfloat16
F32 = jnp.float32
SMEM_SPEC = pl.BlockSpec(memory_space=pltpu.SMEM)
VMEM_SPEC = pl.BlockSpec(memory_space=pltpu.VMEM)
BLK = ("y", "z")
ROW = ("x", "core")


def whole(shape):
    return pl.BlockSpec(shape, lambda *_: (0,) * len(shape))


def in_vmem(value):
    return pltpu.with_memory_space_constraint(value, pltpu.VMEM)


def far_body(y_count, first, *refs):
    if first:
        place, target, far, samples, *send, slot_of, buffer, count, slot_id = refs
    else:
        slot_of, far, samples, *send, buffer = refs
    step = pl.program_id(0)
    pair, far_count, half, width = far.shape
    cols = buffer.shape[2]
    depth = buffer.shape[1] - META
    z_count = depth // (SLOTS * half)

    @pl.when(step == 0)
    def _():
        if first:
            for i in range(y_count * z_count):
                count[i] = 0
            for i in range(y_count * z_count * SLOTS):
                slot_id[i] = -1

        def clear(i, carry):
            start = pl.multiple_of(i * (SLOTS * half), SLOTS * half)
            for d in range(y_count):
                buffer[d, pl.ds(start, SLOTS * half)] = jnp.zeros((SLOTS * half, cols), BF16)
            return carry

        lax.fori_loop(0, z_count, clear, 0)

    for i in range(pair):
        j = step * pair + i
        product = jnp.dot(far[i].reshape(far_count * half, width), samples[i], preferred_element_type=F32)
        product = product.astype(BF16).reshape(far_count, half, cols)
        for k in range(far_count):
            if first:
                local = target.shape[0]
                t = target[j, k]
                h = jnp.clip(t // local, 0, y_count * z_count - 1)
                g = (h // z_count + y_count - place[0]) % y_count * z_count + h % z_count
                c = jnp.minimum(count[g], SLOTS - 1)
                count[g] = c + 1
                q = g * SLOTS + c
                slot_of[j * far_count + k] = q
                slot_id[q] = t % local
            else:
                q = slot_of[j * far_count + k]
            start = pl.multiple_of(q % (z_count * SLOTS) * half, half)
            buffer[q // (z_count * SLOTS), pl.ds(start, half)] = product[k]

    @pl.when(step == pl.num_programs(0) - 1)
    def _():
        if first:
            row = lax.broadcasted_iota(jnp.int32, (META, cols), 0)
            lane = lax.broadcasted_iota(jnp.int32, (META, cols), 1) // (cols // SLOTS)
        for d in range(y_count):
            send[d][:depth] = buffer[d, :depth]
            if first:
                ids = jnp.full(row.shape, -1, jnp.int32)
                for z in range(z_count):
                    for c in range(SLOTS):
                        value = slot_id[(d * z_count + z) * SLOTS + c]
                        ids = jnp.where((row == z) & (lane == c), value, ids)
                send[d][depth:] = ids.astype(F32).astype(BF16)


def far_products(part, far_kernel, samples, y_count, z_count, *scalars):
    local, far_count, rows, width = far_kernel.shape
    cols = samples.shape[2]
    half = rows // 2
    first = part == 0
    depth = z_count * SLOTS * half
    pair = 2
    flops = local * far_count * rows * width * cols
    sends = [jax.ShapeDtypeStruct((depth + (META if first else 0), cols), BF16)] * y_count
    slots = [jax.ShapeDtypeStruct((local * far_count,), jnp.int32)] if first else []
    scratch = [pltpu.VMEM((y_count, depth + META, cols), BF16)]
    if first:
        scratch += [
            pltpu.SMEM((y_count * z_count,), jnp.int32),
            pltpu.SMEM((y_count * z_count * SLOTS,), jnp.int32),
        ]
    return pl.pallas_call(
        functools.partial(far_body, y_count, first),
        grid=(local // pair,),
        in_specs=[SMEM_SPEC] * len(scalars)
        + [
            pl.BlockSpec((pair, far_count, half, width), lambda j: (j, 0, part, 0)),
            pl.BlockSpec((pair, width, cols), lambda j: (j, 0, 0)),
        ],
        out_specs=[VMEM_SPEC] * y_count + [SMEM_SPEC] * len(slots),
        out_shape=sends + slots,
        scratch_shapes=scratch,
        cost_estimate=pl.CostEstimate(flops=flops, bytes_accessed=4000000, transcendentals=0),
        name="far_products_%d" % part,
    )(*scalars, far_kernel, samples)


def near_body(near, samples, minus_near):
    for i in range(2):
        near_sum = jnp.dot(near[i, 0], samples[i], preferred_element_type=F32)
        near_sum += jnp.dot(near[i, 1], samples[1 - i], preferred_element_type=F32)
        minus_near[i] = -near_sum


def near_products(near_kernel, samples):
    local, _, rows, width = near_kernel.shape
    cols = samples.shape[2]
    return pl.pallas_call(
        near_body,
        grid=(local // 2,),
        in_specs=[
            pl.BlockSpec((2, 2, rows, width), lambda j: (j, 0, 0, 0)),
            pl.BlockSpec((2, width, cols), lambda j: (j, 0, 0)),
        ],
        out_specs=pl.BlockSpec((2, rows, cols), lambda j: (j, 0, 0)),
        out_shape=jax.ShapeDtypeStruct((local, rows, cols), F32),
        cost_estimate=pl.CostEstimate(
            flops=4 * local * rows * width * cols, bytes_accessed=2500000, transcendentals=0
        ),
        name="near_products",
    )(near_kernel, samples)


def collect_body(ids, *refs):
    *received, dense, acc0, acc1, acc2, acc3 = refs
    partial = (acc0, acc1, acc2, acc3)
    z_count, height, cols = dense.shape
    local, half = acc0.shape[0] - 1, acc0.shape[1]

    def step(z, carry):
        for acc in partial:
            acc[...] = jnp.zeros_like(acc)
        for d, block in enumerate(received):
            for c in range(SLOTS):
                at = ids[d, z, c]
                at = jnp.where((at < 0) | (at >= local), local, at)
                start = pl.multiple_of((z * SLOTS + c) * half, half)
                partial[c][at] = partial[c][at] + block[pl.ds(start, half)].astype(F32)
        total = acc0[:local] + acc1[:local] + acc2[:local] + acc3[:local]
        dense[z] = total.reshape(height, cols).astype(BF16)
        return carry

    lax.fori_loop(0, z_count, step, 0)


def collect(ids, received, local, half):
    z_count = ids.shape[1]
    cols = received[0].shape[1]
    return pl.pallas_call(
        collect_body,
        in_specs=[SMEM_SPEC] + [VMEM_SPEC] * len(received),
        out_specs=VMEM_SPEC,
        out_shape=jax.ShapeDtypeStruct((z_count, local * half, cols), BF16),
        scratch_shapes=[pltpu.VMEM((local + 1, half, cols), F32)] * SLOTS,
        cost_estimate=pl.CostEstimate(flops=1000000, bytes_accessed=1600000, transcendentals=0),
        name="collect",
    )(ids, *[in_vmem(part) for part in received])


def dense_sum_body(first, second, minus_near, sketch):
    local, rows, cols = sketch.shape
    half = rows // 2
    for i, part in enumerate((first, second)):
        total = minus_near[:, i * half : (i + 1) * half]
        for z in range(part.shape[0]):
            total = total + part[z].astype(F32).reshape(local, half, cols)
        sketch[:, i * half : (i + 1) * half] = total.astype(BF16)


def dense_sum(first, second, minus_near):
    return pl.pallas_call(
        dense_sum_body,
        in_specs=[VMEM_SPEC] * 3,
        out_specs=VMEM_SPEC,
        out_shape=jax.ShapeDtypeStruct(minus_near.shape, BF16),
        cost_estimate=pl.CostEstimate(flops=1000000, bytes_accessed=1500000, transcendentals=0),
        name="dense_sum",
    )(in_vmem(first), in_vmem(second), minus_near)


def basis_body(sketch, basis_half):
    highest = lax.Precision.HIGHEST
    full_width, cols = sketch.shape
    dot = functools.partial(jnp.dot, precision=highest, preferred_element_type=F32)
    values = sketch[...].astype(F32)
    gram = lax.dot_general(
        values, values, (((0,), (0,)), ((), ())), precision=highest, preferred_element_type=F32
    )
    identity = (
        lax.broadcasted_iota(jnp.int32, (cols, cols), 0) == lax.broadcasted_iota(jnp.int32, (cols, cols), 1)
    ).astype(F32)
    trace = jnp.sum(jnp.sum(gram * identity, axis=1, keepdims=True), axis=0, keepdims=True)
    mean_sq = trace / (full_width * cols) + 1e-6
    level = gram / (full_width * cols * mean_sq)
    root = 1.5 * identity - 0.5 * level
    level = dot(level, root)
    for _ in range(ITERS - 2):
        step = 1.5 * identity - 0.5 * dot(root, level)
        level = dot(level, step)
        root = dot(step, root)
    step = 1.5 * identity - 0.5 * dot(root, level)
    root = dot(step, root)
    result = dot(values, root / jnp.sqrt(cols * mean_sq))
    basis_half[...] = result.astype(BF16)


def basis_of(sketch):
    return pl.pallas_call(
        basis_body,
        in_specs=[VMEM_SPEC],
        out_specs=VMEM_SPEC,
        out_shape=jax.ShapeDtypeStruct(sketch.shape, BF16),
        cost_estimate=pl.CostEstimate(flops=2000000000, bytes_accessed=1000000, transcendentals=0),
        name="basis_of",
    )(sketch)


def spread_body(basis, first, second, basis_out):
    local, rows, cols = basis.shape
    half = rows // 2
    for i, part in enumerate((first, second)):
        values = basis[:, i * half : (i + 1) * half].reshape(local * half, cols)
        for z in range(part.shape[0]):
            part[z] = values
    basis_out[...] = basis[...].astype(F32)


def spread(basis, z_count):
    local, rows, cols = basis.shape
    part = jax.ShapeDtypeStruct((z_count, local * rows // 2, cols), BF16)
    return pl.pallas_call(
        spread_body,
        in_specs=[VMEM_SPEC],
        out_specs=[VMEM_SPEC] * 3,
        out_shape=[part, part, jax.ShapeDtypeStruct(basis.shape, F32)],
        cost_estimate=pl.CostEstimate(flops=1000000, bytes_accessed=1500000, transcendentals=0),
        name="spread",
    )(basis)


def pick_body(half, ids, basis, *send):
    z_count, height, _ = basis.shape
    local = height // half

    def step(z, carry):
        for d, block in enumerate(send):
            for c in range(SLOTS):
                at = jnp.clip(ids[d, z, c], 0, local - 1)
                start = pl.multiple_of((z * SLOTS + c) * half, half)
                block[pl.ds(start, half)] = basis[z, pl.ds(pl.multiple_of(at * half, half), half)]
        return carry

    lax.fori_loop(0, z_count, step, 0)


def pick(ids, basis, half):
    y_count, z_count, _ = ids.shape
    cols = basis.shape[2]
    return pl.pallas_call(
        functools.partial(pick_body, half),
        in_specs=[SMEM_SPEC, VMEM_SPEC],
        out_specs=[VMEM_SPEC] * y_count,
        out_shape=[jax.ShapeDtypeStruct((z_count * SLOTS * half, cols), BF16)] * y_count,
        cost_estimate=pl.CostEstimate(flops=1000000, bytes_accessed=1600000, transcendentals=0),
        name="pick",
    )(ids, in_vmem(basis))


def coupling_body(slot_of, place, far, own, across, samples, *refs):
    *received, mine, other, parent, scratch, picked = refs
    j = pl.program_id(0)
    far_count, rows, width = far.shape[1:]
    cols = own.shape[2]
    x_count, _, out_rows, _ = mine.shape
    half = rows // 2
    y_count = picked.shape[1]
    slots = picked.shape[2] // half

    @pl.when(j == 0)
    def _():
        for d in range(y_count):
            picked[0, d] = received[d][...]
            picked[1, d] = received[y_count + d][...]

    core = place[1]
    segment = jnp.where(j % 2 == core, own[0], across[0])
    mixed = jnp.dot(far[0].reshape(far_count * rows, width), segment, preferred_element_type=F32)
    mixed = mixed.astype(BF16).reshape(far_count, rows, cols)
    zero = jnp.zeros((rows, cols), BF16)
    for k in range(0, far_count, 2):
        basis_rows = []
        for i in range(2):
            q = slot_of[j * far_count + k + i]
            start = pl.multiple_of(q % slots * half, half)
            basis_rows.append(picked[0, q // slots, pl.ds(start, half)])
            basis_rows.append(picked[1, q // slots, pl.ds(start, half)])
        right = jnp.concatenate(
            [
                jnp.concatenate([mixed[k], zero], axis=1),
                jnp.concatenate([zero, mixed[k + 1]], axis=1),
            ],
            axis=0,
        )
        both = lax.dot_general(
            jnp.concatenate(basis_rows, axis=0),
            right,
            (((0,), (0,)), ((), ())),
            preferred_element_type=F32,
        )
        for i in range(2):
            part = both[:, i * cols : (i + 1) * cols].reshape(x_count, 2, out_rows, cols)
            mine[:, k + i] = jnp.where(core == 0, part[:, 0], part[:, 1]).astype(BF16)
            other[:, k + i] = jnp.where(core == 0, part[:, 1], part[:, 0]).astype(BF16)

    @pl.when(j % 2 == place[0] // 4)
    def _():
        scratch[...] = lax.dot_general(
            segment, samples[0], (((0,), (0,)), ((), ())), preferred_element_type=F32
        ) / jnp.sqrt(F32(width))
        count = parent.shape[1]
        start = pl.multiple_of((place[0] % 4) * count, count)
        parent[j // 2] = scratch[pl.ds(start, count)]


def coupling_parts(slot_of, place, far_kernel, own, across, received, samples):
    local, far_count, rows, width = far_kernel.shape
    x_count, _, cols = own.shape
    blocks = local * far_count
    out_rows = cols // local
    parent_rows = 2 * cols // local
    flops = 2 * blocks * rows * cols * (width + cols)
    part_spec = pl.BlockSpec((x_count, far_count, out_rows, cols), lambda j, *_: (0, j, 0, 0))
    part_shape = jax.ShapeDtypeStruct((x_count, blocks, out_rows, cols), BF16)
    side = pl.BlockSpec(
        (1, width, cols), lambda j, slots, place: ((place[0] // 2 + x_count - j // 2) % x_count, 0, 0)
    )
    y_count = len(received) // 2
    return pl.pallas_call(
        coupling_body,
        grid_spec=pltpu.PrefetchScalarGridSpec(
            num_scalar_prefetch=2,
            grid=(local,),
            in_specs=[
                pl.BlockSpec((1, far_count, rows, width), lambda j, *_: (j, 0, 0, 0)),
                side,
                side,
                pl.BlockSpec((1, width, cols), lambda j, *_: (j, 0, 0)),
            ]
            + [VMEM_SPEC] * len(received),
            out_specs=[part_spec, part_spec, VMEM_SPEC],
            scratch_shapes=[
                pltpu.VMEM((cols, cols), F32),
                pltpu.VMEM((2, y_count) + received[0].shape, BF16),
            ],
        ),
        out_shape=[part_shape, part_shape, jax.ShapeDtypeStruct((local // 2, parent_rows, cols), F32)],
        cost_estimate=pl.CostEstimate(flops=flops, bytes_accessed=10000000, transcendentals=0),
        name="coupling_parts",
    )(slot_of, place, far_kernel, own, across, samples, *[in_vmem(part) for part in received])


def per_device(far_kernel, near_kernel, samples, far_target):
    local, far_count, rows, width = far_kernel.shape
    cols = samples.shape[2]
    y_count, z_count = lax.axis_size("y"), lax.axis_size("z")
    half = rows // 2
    x_count = lax.axis_size("x")
    core = lax.axis_index("core")
    place = jnp.stack([lax.axis_index("x") * 2 + core, core]).astype(jnp.int32)

    y_place = lax.axis_index("y").astype(jnp.int32).reshape(1)

    def along_y(parts, sign):
        moved = [
            lax.ppermute(parts[d], "y", [(i, (i + sign * d) % y_count) for i in range(y_count)])
            for d in range(1, y_count)
        ]
        return [parts[0]] + moved

    *sent, slot_of = far_products(0, far_kernel, samples, y_count, z_count, y_place, far_target)
    first = along_y(sent, 1)
    later = far_products(1, far_kernel, samples, y_count, z_count, slot_of)
    first, later = lax.optimization_barrier((first, later))
    second = along_y(later, 1)
    minus_near = near_products(near_kernel, samples)
    ids = jnp.stack([part[z_count * SLOTS * half :, :: cols // SLOTS] for part in first]).astype(jnp.int32)
    first, second = [
        lax.all_to_all(collect(ids, part, local, half), "z", 0, 0, tiled=True)
        for part in (first, second)
    ]
    sketch = dense_sum(first, second, minus_near)
    sketch = lax.all_to_all(sketch, ROW, 0, 0, tiled=True)
    basis = basis_of(sketch.reshape(width, cols))
    basis_rows = lax.all_to_all(basis.reshape(local, rows, cols), ROW, 0, 0, tiled=True)
    first, second, basis_out = spread(basis_rows, z_count)
    shifted = [
        lax.ppermute(basis, "x", [(i, (i + d) % x_count) for i in range(x_count)]) for d in range(1, x_count)
    ]
    own = jnp.stack([basis] + shifted)
    first = lax.all_to_all(first, "z", 0, 0, tiled=True)
    first, second, own = lax.optimization_barrier((first, second, own))
    received = along_y(pick(ids, first, half), -1)
    second = lax.all_to_all(second, "z", 0, 0, tiled=True)
    received += along_y(pick(ids, second, half), -1)
    across = lax.ppermute(own, "core", [(0, 1), (1, 0)])
    mine, other, parent = coupling_parts(slot_of, place, far_kernel, own, across, received, samples)
    partner = lax.ppermute(other, "core", [(0, 1), (1, 0)])
    pair = (mine.astype(F32) + partner.astype(F32)).astype(BF16)
    parts = lax.all_to_all(pair, "x", 0, 0, tiled=True)
    coupling = jnp.sum(parts.astype(F32), axis=0) / jnp.sqrt(F32(width))
    return basis_out, coupling.reshape(local, far_count, cols // (2 * x_count), cols), parent


def solution(mesh):
    fine = Mesh(mesh.devices.reshape(4, 8, 4, 2), ("y", "z", "x", "core"))
    return jax.shard_map(
        per_device,
        mesh=fine,
        in_specs=(
            P(BLK, None, ROW, None),
            P(BLK, None, ROW, None),
            P(BLK, None, None),
            P(BLK, None),
        ),
        out_specs=(P(BLK, ROW, None), P(BLK, None, ROW, None), P(BLK, ROW, None)),
        check_vma=False,
    )
```

```python
import functools

import jax
import jax.numpy as jnp
from jax import lax
from jax.experimental import pallas as pl
from jax.experimental.pallas import tpu as pltpu
from jax.sharding import Mesh, PartitionSpec as P

ITERS = 12
SLOTS = 4
META = 8
BF16 = jnp.bfloat16
F32 = jnp.float32
SMEM_SPEC = pl.BlockSpec(memory_space=pltpu.SMEM)
VMEM_SPEC = pl.BlockSpec(memory_space=pltpu.VMEM)
BLK = ("y", "z")
ROW = ("x", "core")


def whole(shape):
    return pl.BlockSpec(shape, lambda *_: (0,) * len(shape))


def in_vmem(value):
    return pltpu.with_memory_space_constraint(value, pltpu.VMEM)


def far_kernel_body(groups, target, far, samples, send, slot_of, count, slot_id):
    step = pl.program_id(0)
    pair, far_count, rows, width = far.shape
    cols = send.shape[2]
    local = target.shape[0]

    @pl.when(step == 0)
    def _():
        for i in range(groups):
            count[i] = 0
        for i in range(groups * SLOTS):
            slot_id[i] = -1

        def clear(h, carry):
            send[h, : SLOTS * rows] = jnp.zeros((SLOTS * rows, cols), BF16)
            return carry

        lax.fori_loop(0, groups, clear, 0)

    for i in range(pair):
        j = step * pair + i
        product = jnp.dot(far[i].reshape(far_count * rows, width), samples[i], preferred_element_type=F32)
        product = product.astype(BF16).reshape(far_count, rows, cols)
        for k in range(far_count):
            t = target[j, k]
            h = jnp.clip(t // local, 0, groups - 1)
            c = jnp.minimum(count[h], SLOTS - 1)
            count[h] = c + 1
            slot_of[j * far_count + k] = h * SLOTS + c
            slot_id[h * SLOTS + c] = t % local
            start = pl.multiple_of(c * rows, rows)
            send[h, pl.ds(start, rows)] = product[k]

    @pl.when(step == pl.num_programs(0) - 1)
    def _():
        row = lax.broadcasted_iota(jnp.int32, (META, cols), 0)

        def header(h, carry):
            ids = jnp.full(row.shape, -1, jnp.int32)
            for c in range(SLOTS):
                ids = jnp.where(row == c, slot_id[h * SLOTS + c], ids)
            send[h, SLOTS * rows :] = ids.astype(F32).astype(BF16)
            return carry

        lax.fori_loop(0, groups, header, 0, unroll=4)


def far_products(far_kernel, samples, far_target, groups):
    local, far_count, rows, width = far_kernel.shape
    cols = samples.shape[2]
    depth = SLOTS * rows + META
    pair = 2
    flops = 2 * local * far_count * rows * width * cols
    return pl.pallas_call(
        functools.partial(far_kernel_body, groups),
        grid=(local // pair,),
        in_specs=[
            SMEM_SPEC,
            pl.BlockSpec((pair, far_count, rows, width), lambda j: (j, 0, 0, 0)),
            pl.BlockSpec((pair, width, cols), lambda j: (j, 0, 0)),
        ],
        out_specs=[VMEM_SPEC, SMEM_SPEC],
        out_shape=[
            jax.ShapeDtypeStruct((groups, depth, cols), BF16),
            jax.ShapeDtypeStruct((local * far_count,), jnp.int32),
        ],
        scratch_shapes=[pltpu.SMEM((groups,), jnp.int32), pltpu.SMEM((groups * SLOTS,), jnp.int32)],
        cost_estimate=pl.CostEstimate(flops=flops, bytes_accessed=7500000, transcendentals=0),
        name="far_products",
    )(far_target, far_kernel, samples)


def near_body(near, samples, minus_near):
    for i in range(2):
        near_sum = jnp.dot(near[i, 0], samples[i], preferred_element_type=F32)
        near_sum += jnp.dot(near[i, 1], samples[1 - i], preferred_element_type=F32)
        minus_near[i] = -near_sum


def near_products(near_kernel, samples):
    local, _, rows, width = near_kernel.shape
    cols = samples.shape[2]
    return pl.pallas_call(
        near_body,
        grid=(local // 2,),
        in_specs=[
            pl.BlockSpec((2, 2, rows, width), lambda j: (j, 0, 0, 0)),
            pl.BlockSpec((2, width, cols), lambda j: (j, 0, 0)),
        ],
        out_specs=pl.BlockSpec((2, rows, cols), lambda j: (j, 0, 0)),
        out_shape=jax.ShapeDtypeStruct((local, rows, cols), F32),
        cost_estimate=pl.CostEstimate(
            flops=4 * local * rows * width * cols, bytes_accessed=2500000, transcendentals=0
        ),
        name="near_products",
    )(near_kernel, samples)


def gather_sum_body(ids, received, minus_near, sketch, *partial):
    local, rows, cols = minus_near.shape
    for acc in partial:
        acc[...] = jnp.zeros_like(acc)

    def step(g, carry):
        for c in range(SLOTS):
            at = ids[g, c]
            at = jnp.where((at < 0) | (at >= local), local, at)
            partial[c][at] = partial[c][at] + received[g, c * rows : (c + 1) * rows].astype(F32)
        return carry

    lax.fori_loop(0, received.shape[0], step, 0)
    total = minus_near[...]
    for acc in partial:
        total = total + acc[:local]
    sketch[...] = total.astype(BF16)


def gather_sum(ids, received, minus_near):
    local, rows, cols = minus_near.shape
    return pl.pallas_call(
        gather_sum_body,
        in_specs=[SMEM_SPEC, VMEM_SPEC, VMEM_SPEC],
        out_specs=VMEM_SPEC,
        out_shape=jax.ShapeDtypeStruct(minus_near.shape, BF16),
        scratch_shapes=[pltpu.VMEM((local + 1, rows, cols), F32)] * SLOTS,
        cost_estimate=pl.CostEstimate(flops=2000000, bytes_accessed=3000000, transcendentals=0),
        name="gather_sum",
    )(ids, received, minus_near)


def split(value):
    high = value.astype(BF16)
    return high, (value - high.astype(F32)).astype(BF16)


def left(parts):
    return jnp.concatenate(parts, axis=1)


def right(parts):
    row = jnp.concatenate(parts, axis=1)
    return jnp.concatenate([row, row], axis=0)


def product(a, b):
    both = jnp.dot(a, b, preferred_element_type=F32)
    cols = both.shape[1] // 2
    return both[:, :cols] + both[:, cols:]


def basis_body(sketch, basis_half):
    full_width, cols = sketch.shape
    values = sketch[...]
    gram = lax.dot_general(values, values, (((0,), (0,)), ((), ())), preferred_element_type=F32)
    identity = (
        lax.broadcasted_iota(jnp.int32, (cols, cols), 0) == lax.broadcasted_iota(jnp.int32, (cols, cols), 1)
    ).astype(F32)
    trace = jnp.sum(jnp.sum(gram * identity, axis=1, keepdims=True), axis=0, keepdims=True)
    mean_sq = trace / (full_width * cols) + 1e-6
    level = gram / (full_width * cols * mean_sq)
    root = 1.5 * identity - 0.5 * level
    step_parts = root_parts = split(root)
    level_parts = split(level)
    for i in range(ITERS - 1):
        level = product(left(level_parts), right(step_parts))
        if i:
            root = product(left(step_parts), right(root_parts))
        level_parts, root_parts = split(level), split(root)
        step_parts = split(1.5 * identity - 0.5 * product(left(root_parts), right(level_parts)))
    root = product(left(step_parts), right(root_parts)) / jnp.sqrt(cols * mean_sq)
    basis_half[...] = product(values, jnp.concatenate(split(root), axis=1)).astype(BF16)


def basis_of(sketch):
    return pl.pallas_call(
        basis_body,
        in_specs=[VMEM_SPEC],
        out_specs=VMEM_SPEC,
        out_shape=jax.ShapeDtypeStruct(sketch.shape, BF16),
        cost_estimate=pl.CostEstimate(flops=500000000, bytes_accessed=1000000, transcendentals=0),
        name="basis_of",
    )(sketch)


def pick_body(ids, basis, send):
    local, rows, _ = basis.shape

    def step(g, carry):
        for c in range(SLOTS):
            at = jnp.clip(ids[g, c], 0, local - 1)
            send[g, c * rows : (c + 1) * rows] = basis[at]
        return carry

    lax.fori_loop(0, send.shape[0], step, 0, unroll=2)


def pick(ids, basis):
    local, rows, cols = basis.shape
    groups = ids.shape[0]
    shape = (groups, SLOTS * rows, cols)
    return pl.pallas_call(
        pick_body,
        in_specs=[SMEM_SPEC, VMEM_SPEC],
        out_specs=VMEM_SPEC,
        out_shape=jax.ShapeDtypeStruct(shape, BF16),
        cost_estimate=pl.CostEstimate(flops=1000000, bytes_accessed=3000000, transcendentals=0),
        name="pick",
    )(ids, basis)


def mixed_body(place, far, own, across, samples, mixed, parent, scratch):
    j = pl.program_id(0)
    far_count, rows, width = far.shape[1:]
    cols = own.shape[2]
    segment = jnp.where(j % 2 == place[0] % 2, own[0], across[0])
    values = jnp.dot(far[0].reshape(far_count * rows, width), segment, preferred_element_type=F32)
    mixed[...] = values.astype(BF16).reshape(far_count, rows, cols)

    @pl.when(j % 2 == place[0] // 4)
    def _():
        scratch[...] = lax.dot_general(
            segment, samples[0], (((0,), (0,)), ((), ())), preferred_element_type=F32
        ) / jnp.sqrt(F32(width))
        count = parent.shape[1]
        start = pl.multiple_of((place[0] % 4) * count, count)
        parent[j // 2] = scratch[pl.ds(start, count)]


def mixed_products(place, far_kernel, own, across, samples):
    local, far_count, rows, width = far_kernel.shape
    x_count, _, cols = own.shape
    parent_rows = 2 * cols // local
    side = pl.BlockSpec(
        (1, width, cols), lambda j, place: ((place[0] // 2 + x_count - j // 2) % x_count, 0, 0)
    )
    return pl.pallas_call(
        mixed_body,
        grid_spec=pltpu.PrefetchScalarGridSpec(
            num_scalar_prefetch=1,
            grid=(local,),
            in_specs=[
                pl.BlockSpec((1, far_count, rows, width), lambda j, *_: (j, 0, 0, 0)),
                side,
                side,
                pl.BlockSpec((1, width, cols), lambda j, *_: (j, 0, 0)),
            ],
            out_specs=[pl.BlockSpec((far_count, rows, cols), lambda j, *_: (j, 0, 0)), VMEM_SPEC],
            scratch_shapes=[pltpu.VMEM((cols, cols), F32)],
        ),
        out_shape=[
            jax.ShapeDtypeStruct((local * far_count, rows, cols), BF16),
            jax.ShapeDtypeStruct((local // 2, parent_rows, cols), F32),
        ],
        cost_estimate=pl.CostEstimate(
            flops=2 * local * far_count * rows * cols * width, bytes_accessed=8000000, transcendentals=0
        ),
        name="mixed_products",
    )(place, far_kernel, own, across, samples)


def coupling_body(base, slot_of, place, mixed, picked, mine, other):
    x_count, blocks, out_rows, cols = mine.shape
    rows = mixed.shape[1]
    zero = jnp.zeros((rows, cols), BF16)
    core = place[0] % 2
    for b in range(0, blocks, 2):
        basis_rows = []
        for i in range(2):
            q = slot_of[base + b + i]
            start = pl.multiple_of((q % SLOTS) * rows, rows)
            basis_rows.append(picked[q // SLOTS, pl.ds(start, rows)])
        diagonal = jnp.concatenate(
            [
                jnp.concatenate([mixed[base + b], zero], axis=1),
                jnp.concatenate([zero, mixed[base + b + 1]], axis=1),
            ],
            axis=0,
        )
        both = lax.dot_general(
            jnp.concatenate(basis_rows, axis=0),
            diagonal,
            (((0,), (0,)), ((), ())),
            preferred_element_type=F32,
        )
        for i in range(2):
            part = both[:, i * cols : (i + 1) * cols].reshape(x_count, 2, out_rows, cols)
            for x in range(x_count):
                d = (x + x_count - place[0] // 2) % x_count
                mine[d, b + i] = jnp.where(core == 0, part[x, 0], part[x, 1]).astype(BF16)
                other[d, b + i] = jnp.where(core == 0, part[x, 1], part[x, 0]).astype(BF16)


def coupling_parts(half, slot_of, place, mixed, picked, x_count, local):
    blocks, rows, cols = mixed.shape
    shape = jax.ShapeDtypeStruct((x_count, blocks // 2, cols // local, cols), BF16)
    return pl.pallas_call(
        functools.partial(coupling_body, half * blocks // 2),
        in_specs=[SMEM_SPEC, SMEM_SPEC, VMEM_SPEC, VMEM_SPEC],
        out_specs=[VMEM_SPEC, VMEM_SPEC],
        out_shape=[shape, shape],
        cost_estimate=pl.CostEstimate(
            flops=2 * blocks * rows * cols * cols, bytes_accessed=4000000, transcendentals=0
        ),
        name="coupling_parts_%d" % half,
    )(slot_of, place, mixed, in_vmem(picked) if half == 0 else picked)


def per_device(far_kernel, near_kernel, samples, far_target):
    local, far_count, rows, width = far_kernel.shape
    cols = samples.shape[2]
    groups = lax.axis_size("y") * lax.axis_size("z")
    x_count = lax.axis_size("x")
    place = (lax.axis_index("x") * 2 + lax.axis_index("core")).astype(jnp.int32).reshape(1)

    def along_x(value, d):
        return lax.ppermute(value, "x", [(i, (i + d) % x_count) for i in range(x_count)])

    send, slot_of = far_products(far_kernel, samples, far_target, groups)
    received = lax.all_to_all(send, BLK, 0, 0, tiled=True)
    minus_near = near_products(near_kernel, samples)
    ids = received[:, SLOTS * rows :, 0].astype(jnp.int32)
    received = in_vmem(received)
    sketch = gather_sum(ids, received, minus_near)
    sketch = lax.all_to_all(sketch, ROW, 0, 0, tiled=True)
    basis = basis_of(sketch.reshape(width, cols))
    basis_rows = lax.all_to_all(basis.reshape(local, rows, cols), ROW, 0, 0, tiled=True)
    picked = lax.all_to_all(pick(ids, basis_rows), BLK, 0, 0, tiled=True)
    basis_out = basis_rows.astype(F32)
    own = jnp.stack([basis] + [along_x(basis, d) for d in range(1, x_count)])
    across = lax.ppermute(own, "core", [(0, 1), (1, 0)])
    mixed, parent = mixed_products(place, far_kernel, own, across, samples)
    coupling = []
    for part in range(2):
        mine, other = coupling_parts(part, slot_of, place, mixed, picked, x_count, local)
        partner = lax.ppermute(other, "core", [(0, 1), (1, 0)])
        pair = [mine[d].astype(F32) + partner[d].astype(F32) for d in range(x_count)]
        total = pair[0]
        for d in range(1, x_count):
            total = total + along_x(pair[d].astype(BF16), d).astype(F32)
        coupling.append(total / jnp.sqrt(F32(width)))
    coupling = jnp.concatenate(coupling, axis=0)
    return basis_out, coupling.reshape(local, far_count, cols // local, cols), parent


def solution(mesh):
    fine = Mesh(mesh.devices.reshape(4, 8, 4, 2), ("y", "z", "x", "core"))
    return jax.shard_map(
        per_device,
        mesh=fine,
        in_specs=(
            P(BLK, None, ROW, None),
            P(BLK, None, ROW, None),
            P(BLK, None, None),
            P(BLK, None),
        ),
        out_specs=(P(BLK, ROW, None), P(BLK, None, ROW, None), P(BLK, ROW, None)),
        check_vma=False,
    )
```

```python
import functools

import jax
import jax.numpy as jnp
from jax import lax
from jax.experimental import pallas as pl
from jax.experimental.pallas import tpu as pltpu
from jax.sharding import Mesh, PartitionSpec as P

ITERS = 12
SLOTS = 4
META = 8
BF16 = jnp.bfloat16
F32 = jnp.float32
SMEM_SPEC = pl.BlockSpec(memory_space=pltpu.SMEM)
VMEM_SPEC = pl.BlockSpec(memory_space=pltpu.VMEM)
HBM_SPEC = pl.BlockSpec(memory_space=pl.ANY)
BLK = ("y", "z")
ROW = ("x", "core")


def whole(shape):
    return pl.BlockSpec(shape, lambda *_: (0,) * len(shape))


def in_vmem(value):
    return pltpu.with_memory_space_constraint(value, pltpu.VMEM)


def far_body(groups, target, far, samples, send, slot_of, blocks, columns, staged, header, count, slot_id, in_sem, out_sem, header_sem):
    local, far_count, rows, width = far.shape
    cols = send.shape[2]
    arriving = []
    for j in range(local):
        pieces = [
            pltpu.make_async_copy(far.at[j], blocks.at[j], in_sem.at[0, j]),
            pltpu.make_async_copy(samples.at[j], columns.at[j], in_sem.at[1, j]),
        ]
        for piece in pieces:
            piece.start()
        arriving.append(pieces)
    for i in range(groups):
        count[i] = 0
    for i in range(groups * SLOTS):
        slot_id[i] = -1

    for j in range(local):
        for k in range(far_count):
            t = target[j, k]
            h = jnp.clip(t // local, 0, groups - 1)
            c = jnp.minimum(count[h], SLOTS - 1)
            count[h] = c + 1
            slot_of[j * far_count + k] = h * SLOTS + c
            slot_id[h * SLOTS + c] = t % local
        for piece in arriving[j]:
            piece.wait()
        product = jnp.dot(
            blocks[j].reshape(far_count * rows, width), columns[j], preferred_element_type=F32
        )
        staged[j * far_count : (j + 1) * far_count] = product.astype(BF16).reshape(far_count, rows, cols)
        for k in range(far_count):
            q = slot_of[j * far_count + k]
            start = pl.multiple_of(q % SLOTS * rows, rows)
            pltpu.make_async_copy(
                staged.at[j * far_count + k], send.at[q // SLOTS, pl.ds(start, rows)], out_sem
            ).start()

    row = lax.broadcasted_iota(jnp.int32, (META, cols), 0)

    def write_header(h, carry):
        ids = jnp.full(row.shape, -1, jnp.int32)
        for c in range(SLOTS):
            ids = jnp.where(row == c, slot_id[h * SLOTS + c], ids)
        header[h] = ids.astype(F32).astype(BF16)
        return carry

    lax.fori_loop(0, groups, write_header, 0, unroll=4)
    last = pltpu.make_async_copy(header, send.at[:, pl.ds(SLOTS * rows, META)], header_sem)
    last.start()
    last.wait()
    pltpu.make_async_copy(staged, staged, out_sem).wait()


def far_products(far_kernel, samples, far_target, groups):
    local, far_count, rows, width = far_kernel.shape
    cols = samples.shape[2]
    depth = SLOTS * rows + META
    flops = 2 * local * far_count * rows * width * cols
    return pl.pallas_call(
        functools.partial(far_body, groups),
        in_specs=[SMEM_SPEC, HBM_SPEC, HBM_SPEC],
        out_specs=[HBM_SPEC, SMEM_SPEC],
        out_shape=[
            jax.ShapeDtypeStruct((groups, depth, cols), BF16),
            jax.ShapeDtypeStruct((local * far_count,), jnp.int32),
        ],
        scratch_shapes=[
            pltpu.VMEM(far_kernel.shape, BF16),
            pltpu.VMEM(samples.shape, BF16),
            pltpu.VMEM((local * far_count, rows, cols), BF16),
            pltpu.VMEM((groups, META, cols), BF16),
            pltpu.SMEM((groups,), jnp.int32),
            pltpu.SMEM((groups * SLOTS,), jnp.int32),
            pltpu.SemaphoreType.DMA((2, local)),
            pltpu.SemaphoreType.DMA,
            pltpu.SemaphoreType.DMA,
        ],
        cost_estimate=pl.CostEstimate(flops=flops, bytes_accessed=7500000, transcendentals=0),
        name="far_products",
    )(far_target, far_kernel, samples)


def near_body(near, samples, minus_near):
    for i in range(2):
        near_sum = jnp.dot(near[i, 0], samples[i], preferred_element_type=F32)
        near_sum += jnp.dot(near[i, 1], samples[1 - i], preferred_element_type=F32)
        minus_near[i] = -near_sum


def near_products(near_kernel, samples):
    local, _, rows, width = near_kernel.shape
    cols = samples.shape[2]
    return pl.pallas_call(
        near_body,
        grid=(local // 2,),
        in_specs=[
            pl.BlockSpec((2, 2, rows, width), lambda j: (j, 0, 0, 0)),
            pl.BlockSpec((2, width, cols), lambda j: (j, 0, 0)),
        ],
        out_specs=pl.BlockSpec((2, rows, cols), lambda j: (j, 0, 0)),
        out_shape=jax.ShapeDtypeStruct((local, rows, cols), F32),
        cost_estimate=pl.CostEstimate(
            flops=4 * local * rows * width * cols, bytes_accessed=2500000, transcendentals=0
        ),
        name="near_products",
    )(near_kernel, samples)


def gather_sum_body(ids, received, minus_near, sketch, *partial):
    local, rows, cols = minus_near.shape
    for acc in partial:
        acc[...] = jnp.zeros_like(acc)

    def step(g, carry):
        for c in range(SLOTS):
            at = ids[g, c]
            at = jnp.where((at < 0) | (at >= local), local, at)
            partial[c][at] = partial[c][at] + received[g, c * rows : (c + 1) * rows].astype(F32)
        return carry

    lax.fori_loop(0, received.shape[0], step, 0, unroll=4)
    total = minus_near[...]
    for acc in partial:
        total = total + acc[:local]
    sketch[...] = total.astype(BF16)


def gather_sum(ids, received, minus_near):
    local, rows, cols = minus_near.shape
    return pl.pallas_call(
        gather_sum_body,
        in_specs=[SMEM_SPEC, VMEM_SPEC, VMEM_SPEC],
        out_specs=VMEM_SPEC,
        out_shape=jax.ShapeDtypeStruct(minus_near.shape, BF16),
        scratch_shapes=[pltpu.VMEM((local + 1, rows, cols), F32)] * SLOTS,
        cost_estimate=pl.CostEstimate(flops=2000000, bytes_accessed=3000000, transcendentals=0),
        name="gather_sum",
    )(ids, received, minus_near)


def split(value):
    high = value.astype(BF16)
    return high, (value - high.astype(F32)).astype(BF16)


def left(parts):
    return jnp.concatenate(parts, axis=1)


def right(parts):
    row = jnp.concatenate(parts, axis=1)
    return jnp.concatenate([row, row], axis=0)


def product(a, b):
    both = jnp.dot(a, b, preferred_element_type=F32)
    cols = both.shape[1] // 2
    return both[:, :cols] + both[:, cols:]


def basis_body(sketch, basis_half):
    full_width, cols = sketch.shape
    values = sketch[...]
    gram = lax.dot_general(values, values, (((0,), (0,)), ((), ())), preferred_element_type=F32)
    identity = (
        lax.broadcasted_iota(jnp.int32, (cols, cols), 0) == lax.broadcasted_iota(jnp.int32, (cols, cols), 1)
    ).astype(F32)
    trace = jnp.sum(jnp.sum(gram * identity, axis=1, keepdims=True), axis=0, keepdims=True)
    mean_sq = trace / (full_width * cols) + 1e-6
    level = gram / (full_width * cols * mean_sq)
    root = 1.5 * identity - 0.5 * level
    step_parts = root_parts = split(root)
    level_parts = split(level)
    for i in range(ITERS - 1):
        level = product(left(level_parts), right(step_parts))
        if i:
            root = product(left(step_parts), right(root_parts))
        level_parts, root_parts = split(level), split(root)
        step_parts = split(1.5 * identity - 0.5 * product(left(root_parts), right(level_parts)))
    root = product(left(step_parts), right(root_parts)) / jnp.sqrt(cols * mean_sq)
    basis_half[...] = product(values, jnp.concatenate(split(root), axis=1)).astype(BF16)


def basis_of(sketch):
    return pl.pallas_call(
        basis_body,
        in_specs=[VMEM_SPEC],
        out_specs=VMEM_SPEC,
        out_shape=jax.ShapeDtypeStruct(sketch.shape, BF16),
        cost_estimate=pl.CostEstimate(flops=500000000, bytes_accessed=1000000, transcendentals=0),
        name="basis_of",
    )(sketch)


def pick_body(ids, basis, send, sem):
    local, rows, _ = basis.shape

    def step(g, carry):
        for c in range(SLOTS):
            at = jnp.clip(ids[g, c], 0, local - 1)
            pltpu.make_async_copy(basis.at[at], send.at[g, pl.ds(c * rows, rows)], sem).start()
        return carry

    lax.fori_loop(0, send.shape[0], step, 0, unroll=2)
    pltpu.make_async_copy(send, send, sem).wait()


def pick(ids, basis):
    local, rows, cols = basis.shape
    groups = ids.shape[0]
    shape = (groups, SLOTS * rows, cols)
    return pl.pallas_call(
        pick_body,
        in_specs=[SMEM_SPEC, VMEM_SPEC],
        out_specs=HBM_SPEC,
        out_shape=jax.ShapeDtypeStruct(shape, BF16),
        scratch_shapes=[pltpu.SemaphoreType.DMA],
        cost_estimate=pl.CostEstimate(flops=1000000, bytes_accessed=3000000, transcendentals=0),
        name="pick",
    )(ids, basis)


def mixed_body(place, far, own, across, samples, mixed, parent, scratch):
    j = pl.program_id(0)
    far_count, rows, width = far.shape[1:]
    cols = own.shape[2]
    segment = jnp.where(j % 2 == place[0] % 2, own[0], across[0])
    values = jnp.dot(far[0].reshape(far_count * rows, width), segment, preferred_element_type=F32)
    mixed[pl.ds(j * far_count, far_count)] = values.astype(BF16).reshape(far_count, rows, cols)

    @pl.when(j % 2 == place[0] // 4)
    def _():
        scratch[...] = lax.dot_general(
            segment, samples[0], (((0,), (0,)), ((), ())), preferred_element_type=F32
        ) / jnp.sqrt(F32(width))
        count = parent.shape[1]
        start = pl.multiple_of((place[0] % 4) * count, count)
        parent[j // 2] = scratch[pl.ds(start, count)]


def mixed_products(place, far_kernel, own, across, samples):
    local, far_count, rows, width = far_kernel.shape
    x_count, _, cols = own.shape
    parent_rows = 2 * cols // local
    side = pl.BlockSpec(
        (1, width, cols), lambda j, place: ((place[0] // 2 + x_count - j // 2) % x_count, 0, 0)
    )
    return pl.pallas_call(
        mixed_body,
        grid_spec=pltpu.PrefetchScalarGridSpec(
            num_scalar_prefetch=1,
            grid=(local,),
            in_specs=[
                pl.BlockSpec((1, far_count, rows, width), lambda j, *_: (j, 0, 0, 0)),
                side,
                side,
                pl.BlockSpec((1, width, cols), lambda j, *_: (j, 0, 0)),
            ],
            out_specs=[VMEM_SPEC, VMEM_SPEC],
            scratch_shapes=[pltpu.VMEM((cols, cols), F32)],
        ),
        out_shape=[
            pltpu.VMEM((local * far_count, rows, cols), BF16),
            jax.ShapeDtypeStruct((local // 2, parent_rows, cols), F32),
        ],
        cost_estimate=pl.CostEstimate(
            flops=2 * local * far_count * rows * cols * width, bytes_accessed=8000000, transcendentals=0
        ),
        name="mixed_products",
    )(place, far_kernel, own, across, samples)


def coupling_body(base, slot_of, place, mixed, picked, mine, other, *_):
    x_count, blocks, out_rows, cols = mine.shape
    rows = mixed.shape[1]
    zero = jnp.zeros((rows, cols), BF16)
    core = place[0] % 2
    for b in range(0, blocks, 2):
        basis_rows = []
        for i in range(2):
            q = slot_of[base + b + i]
            start = pl.multiple_of((q % SLOTS) * rows, rows)
            basis_rows.append(picked[q // SLOTS, pl.ds(start, rows)])
        diagonal = jnp.concatenate(
            [
                jnp.concatenate([mixed[base + b], zero], axis=1),
                jnp.concatenate([zero, mixed[base + b + 1]], axis=1),
            ],
            axis=0,
        )
        both = lax.dot_general(
            jnp.concatenate(basis_rows, axis=0),
            diagonal,
            (((0,), (0,)), ((), ())),
            preferred_element_type=F32,
        )
        for i in range(2):
            part = both[:, i * cols : (i + 1) * cols].reshape(x_count, 2, out_rows, cols)
            for x in range(x_count):
                d = (x + x_count - place[0] // 2) % x_count
                mine[d, b + i] = jnp.where(core == 0, part[x, 0], part[x, 1]).astype(BF16)
                other[d, b + i] = jnp.where(core == 0, part[x, 1], part[x, 0]).astype(BF16)


def coupling_parts(half, slot_of, place, mixed, picked, x_count, local):
    blocks, rows, cols = mixed.shape
    shape = jax.ShapeDtypeStruct((x_count, blocks // 2, cols // local, cols), BF16)
    again = [pltpu.VMEM(picked.shape, BF16)] if half == 0 else []
    return pl.pallas_call(
        functools.partial(coupling_body, half * blocks // 2),
        in_specs=[SMEM_SPEC, SMEM_SPEC, VMEM_SPEC, VMEM_SPEC],
        out_specs=[VMEM_SPEC] * (2 + len(again)),
        out_shape=[shape, shape] + again,
        input_output_aliases={3: 2} if again else {},
        cost_estimate=pl.CostEstimate(
            flops=2 * blocks * rows * cols * cols, bytes_accessed=4000000, transcendentals=0
        ),
        name="coupling_parts_%d" % half,
    )(slot_of, place, in_vmem(mixed), in_vmem(picked))


def finish_body(scale, *refs):
    total = refs[0][...]
    for moved in refs[1:4]:
        total = total + moved[...].astype(F32)
    refs[-1][...] = total * scale


def finish(half, scale, parts, result):
    blocks, rows, cols = parts[0].shape
    before = [] if result is None else [result]
    return pl.pallas_call(
        functools.partial(finish_body, scale),
        grid=(1,),
        in_specs=[VMEM_SPEC] * len(parts) + [HBM_SPEC] * len(before),
        out_specs=pl.BlockSpec(parts[0].shape, lambda i: (half, 0, 0)),
        out_shape=jax.ShapeDtypeStruct((2 * blocks, rows, cols), F32),
        input_output_aliases={len(parts): 0} if before else {},
        cost_estimate=pl.CostEstimate(flops=1000000, bytes_accessed=1000000, transcendentals=0),
        name="finish_%d" % half,
    )(*[in_vmem(part) for part in parts], *before)


def per_device(far_kernel, near_kernel, samples, far_target):
    local, far_count, rows, width = far_kernel.shape
    cols = samples.shape[2]
    groups = lax.axis_size("y") * lax.axis_size("z")
    x_count = lax.axis_size("x")
    place = (lax.axis_index("x") * 2 + lax.axis_index("core")).astype(jnp.int32).reshape(1)

    def along_x(value, d):
        return lax.ppermute(value, "x", [(i, (i + d) % x_count) for i in range(x_count)])

    send, slot_of = far_products(far_kernel, samples, far_target, groups)
    received = lax.all_to_all(send, BLK, 0, 0, tiled=True)
    minus_near = near_products(near_kernel, samples)
    ids = received[:, SLOTS * rows :, 0].astype(jnp.int32)
    received = in_vmem(received)
    sketch = gather_sum(ids, received, minus_near)
    sketch = lax.all_to_all(sketch, ROW, 0, 0, tiled=True)
    basis = basis_of(sketch.reshape(width, cols))
    basis_rows = lax.all_to_all(basis.reshape(local, rows, cols), ROW, 0, 0, tiled=True)
    picked = lax.all_to_all(pick(ids, basis_rows), BLK, 0, 0, tiled=True)
    own = jnp.stack([basis] + [along_x(basis, d) for d in range(1, x_count)])
    own, basis_out = lax.optimization_barrier((own, basis_rows.astype(F32)))
    across = lax.ppermute(own, "core", [(0, 1), (1, 0)])
    mixed, parent = mixed_products(place, far_kernel, own, across, samples)
    coupling = None
    for part in range(2):
        mine, other, *again = coupling_parts(part, slot_of, place, mixed, picked, x_count, local)
        picked = again[0] if again else None
        partner = lax.ppermute(other, "core", [(0, 1), (1, 0)])
        pair = [mine[d].astype(F32) + partner[d].astype(F32) for d in range(x_count)]
        parts = [pair[0]] + [along_x(pair[d].astype(BF16), d) for d in range(1, x_count)]
        coupling = finish(part, width**-0.5, parts, coupling)
    return basis_out, coupling.reshape(local, far_count, cols // local, cols), parent


def solution(mesh):
    fine = Mesh(mesh.devices.reshape(4, 8, 4, 2), ("y", "z", "x", "core"))
    return jax.shard_map(
        per_device,
        mesh=fine,
        in_specs=(
            P(BLK, None, ROW, None),
            P(BLK, None, ROW, None),
            P(BLK, None, None),
            P(BLK, None),
        ),
        out_specs=(P(BLK, ROW, None), P(BLK, None, ROW, None), P(BLK, ROW, None)),
        check_vma=False,
    )
```

```python
import functools

import jax
import jax.numpy as jnp
from jax import lax
from jax.experimental import pallas as pl
from jax.experimental.pallas import tpu as pltpu
from jax.sharding import Mesh, PartitionSpec as P

ITERS = 12
SLOTS = 4
META = 8
BF16 = jnp.bfloat16
F32 = jnp.float32
SMEM_SPEC = pl.BlockSpec(memory_space=pltpu.SMEM)
VMEM_SPEC = pl.BlockSpec(memory_space=pltpu.VMEM)
HBM_SPEC = pl.BlockSpec(memory_space=pl.ANY)
BLK = ("y", "z")
ROW = ("x", "core")


def whole(shape):
    return pl.BlockSpec(shape, lambda *_: (0,) * len(shape))


def in_vmem(value):
    return pltpu.with_memory_space_constraint(value, pltpu.VMEM)


def far_kernel_body(groups, target, far, samples, send, slot_of, count, slot_id):
    step = pl.program_id(0)
    pair, far_count, rows, width = far.shape
    cols = send.shape[2]
    local = target.shape[0]

    @pl.when(step == 0)
    def _():
        for i in range(groups):
            count[i] = 0
        for i in range(groups * SLOTS):
            slot_id[i] = -1

    for i in range(pair):
        j = step * pair + i
        product = jnp.dot(far[i].reshape(far_count * rows, width), samples[i], preferred_element_type=F32)
        product = product.astype(BF16).reshape(far_count, rows, cols)
        for k in range(far_count):
            t = target[j, k]
            h = jnp.clip(t // local, 0, groups - 1)
            c = jnp.minimum(count[h], SLOTS - 1)
            count[h] = c + 1
            slot_of[j * far_count + k] = h * SLOTS + c
            slot_id[h * SLOTS + c] = t % local
            start = pl.multiple_of(c * rows, rows)
            send[h, pl.ds(start, rows)] = product[k]

    @pl.when(step == pl.num_programs(0) - 1)
    def _():
        row = lax.broadcasted_iota(jnp.int32, (META, cols), 0)

        def header(h, carry):
            ids = jnp.full(row.shape, -1, jnp.int32)
            for c in range(SLOTS):
                ids = jnp.where(row == c, slot_id[h * SLOTS + c], ids)
            send[h, SLOTS * rows :] = ids.astype(F32).astype(BF16)
            return carry

        lax.fori_loop(0, groups, header, 0, unroll=4)


def far_products(far_kernel, samples, far_target, groups):
    local, far_count, rows, width = far_kernel.shape
    cols = samples.shape[2]
    depth = SLOTS * rows + META
    pair = 2
    flops = 2 * local * far_count * rows * width * cols
    return pl.pallas_call(
        functools.partial(far_kernel_body, groups),
        grid=(local // pair,),
        in_specs=[
            SMEM_SPEC,
            pl.BlockSpec((pair, far_count, rows, width), lambda j: (j, 0, 0, 0)),
            pl.BlockSpec((pair, width, cols), lambda j: (j, 0, 0)),
        ],
        out_specs=[VMEM_SPEC, SMEM_SPEC],
        out_shape=[
            jax.ShapeDtypeStruct((groups, depth, cols), BF16),
            jax.ShapeDtypeStruct((local * far_count,), jnp.int32),
        ],
        scratch_shapes=[pltpu.SMEM((groups,), jnp.int32), pltpu.SMEM((groups * SLOTS,), jnp.int32)],
        cost_estimate=pl.CostEstimate(flops=flops, bytes_accessed=7500000, transcendentals=0),
        name="far_products",
    )(far_target, far_kernel, samples)


def near_body(near, samples, minus_near):
    for i in range(2):
        near_sum = jnp.dot(near[i, 0], samples[i], preferred_element_type=F32)
        near_sum += jnp.dot(near[i, 1], samples[1 - i], preferred_element_type=F32)
        minus_near[i] = -near_sum


def near_products(near_kernel, samples):
    local, _, rows, width = near_kernel.shape
    cols = samples.shape[2]
    return pl.pallas_call(
        near_body,
        grid=(local // 2,),
        in_specs=[
            pl.BlockSpec((2, 2, rows, width), lambda j: (j, 0, 0, 0)),
            pl.BlockSpec((2, width, cols), lambda j: (j, 0, 0)),
        ],
        out_specs=pl.BlockSpec((2, rows, cols), lambda j: (j, 0, 0)),
        out_shape=jax.ShapeDtypeStruct((local, rows, cols), F32),
        cost_estimate=pl.CostEstimate(
            flops=4 * local * rows * width * cols, bytes_accessed=2500000, transcendentals=0
        ),
        name="near_products",
    )(near_kernel, samples)


def gather_sum_body(ids, received, minus_near, sketch, *partial):
    local, rows, cols = minus_near.shape
    for acc in partial:
        acc[...] = jnp.zeros_like(acc)

    def step(g, carry):
        for c in range(SLOTS):
            at = ids[g, c]
            at = jnp.where((at < 0) | (at >= local), local, at)
            partial[c][at] = partial[c][at] + received[g, c * rows : (c + 1) * rows].astype(F32)
        return carry

    lax.fori_loop(0, received.shape[0], step, 0, unroll=4)
    total = minus_near[...]
    for acc in partial:
        total = total + acc[:local]
    sketch[...] = total.astype(BF16)


def gather_sum(ids, received, minus_near):
    local, rows, cols = minus_near.shape
    return pl.pallas_call(
        gather_sum_body,
        in_specs=[SMEM_SPEC, VMEM_SPEC, VMEM_SPEC],
        out_specs=VMEM_SPEC,
        out_shape=pltpu.VMEM(minus_near.shape, BF16),
        scratch_shapes=[pltpu.VMEM((local + 1, rows, cols), F32)] * SLOTS,
        cost_estimate=pl.CostEstimate(flops=2000000, bytes_accessed=3000000, transcendentals=0),
        name="gather_sum",
    )(ids, received, minus_near)


def split(value):
    high = value.astype(BF16)
    return high, (value - high.astype(F32)).astype(BF16)


def left(parts):
    return jnp.concatenate(parts, axis=1)


def right(parts):
    row = jnp.concatenate(parts, axis=1)
    return jnp.concatenate([row, row], axis=0)


def product(a, b):
    both = jnp.dot(a, b, preferred_element_type=F32)
    cols = both.shape[1] // 2
    return both[:, :cols] + both[:, cols:]


def basis_body(sketch, basis_rows, basis_half):
    full_width, cols = basis_half.shape
    values = sketch[...].reshape(full_width, cols)
    gram = lax.dot_general(values, values, (((0,), (0,)), ((), ())), preferred_element_type=F32)
    identity = (
        lax.broadcasted_iota(jnp.int32, (cols, cols), 0) == lax.broadcasted_iota(jnp.int32, (cols, cols), 1)
    ).astype(F32)
    trace = jnp.sum(jnp.sum(gram * identity, axis=1, keepdims=True), axis=0, keepdims=True)
    mean_sq = trace / (full_width * cols) + 1e-6
    level = gram / (full_width * cols * mean_sq)
    root = 1.5 * identity - 0.5 * level
    step_parts = root_parts = split(root)
    level_parts = split(level)
    for i in range(ITERS - 1):
        level = product(left(level_parts), right(step_parts))
        if i:
            root = product(left(step_parts), right(root_parts))
        level_parts, root_parts = split(level), split(root)
        step_parts = split(1.5 * identity - 0.5 * product(left(root_parts), right(level_parts)))
    root = product(left(step_parts), right(root_parts)) / jnp.sqrt(cols * mean_sq)
    result = product(values, jnp.concatenate(split(root), axis=1)).astype(BF16)
    basis_half[...] = result
    basis_rows[...] = result.reshape(basis_rows.shape)


def basis_of(sketch):
    local, rows, cols = sketch.shape
    return pl.pallas_call(
        basis_body,
        in_specs=[VMEM_SPEC],
        out_specs=[VMEM_SPEC] * 2,
        out_shape=[pltpu.VMEM(sketch.shape, BF16), jax.ShapeDtypeStruct((local * rows, cols), BF16)],
        cost_estimate=pl.CostEstimate(flops=500000000, bytes_accessed=1000000, transcendentals=0),
        name="basis_of",
    )(in_vmem(sketch))


def pick_body(ids, basis, send, sem):
    local, rows, _ = basis.shape

    def step(g, carry):
        for c in range(SLOTS):
            at = jnp.clip(ids[g, c], 0, local - 1)
            pltpu.make_async_copy(basis.at[at], send.at[g, pl.ds(c * rows, rows)], sem).start()
        return carry

    lax.fori_loop(0, send.shape[0], step, 0, unroll=2)
    pltpu.make_async_copy(send, send, sem).wait()


def pick(ids, basis):
    local, rows, cols = basis.shape
    groups = ids.shape[0]
    shape = (groups, SLOTS * rows, cols)
    return pl.pallas_call(
        pick_body,
        in_specs=[SMEM_SPEC, VMEM_SPEC],
        out_specs=HBM_SPEC,
        out_shape=jax.ShapeDtypeStruct(shape, BF16),
        scratch_shapes=[pltpu.SemaphoreType.DMA],
        cost_estimate=pl.CostEstimate(flops=1000000, bytes_accessed=3000000, transcendentals=0),
        name="pick",
    )(ids, in_vmem(basis))


def mixed_body(place, far, own, across, samples, mixed, parent, scratch):
    j = pl.program_id(0)
    far_count, rows, width = far.shape[1:]
    cols = own.shape[2]
    segment = jnp.where(j % 2 == place[0] % 2, own[0], across[0])
    values = jnp.dot(far[0].reshape(far_count * rows, width), segment, preferred_element_type=F32)
    mixed[pl.ds(j * far_count, far_count)] = values.astype(BF16).reshape(far_count, rows, cols)

    @pl.when(j % 2 == place[0] // 4)
    def _():
        scratch[...] = lax.dot_general(
            segment, samples[0], (((0,), (0,)), ((), ())), preferred_element_type=F32
        ) / jnp.sqrt(F32(width))
        count = parent.shape[1]
        start = pl.multiple_of((place[0] % 4) * count, count)
        parent[j // 2] = scratch[pl.ds(start, count)]


def mixed_products(place, far_kernel, own, across, samples):
    local, far_count, rows, width = far_kernel.shape
    x_count, _, cols = own.shape
    parent_rows = 2 * cols // local
    side = pl.BlockSpec(
        (1, width, cols), lambda j, place: ((place[0] // 2 + x_count - j // 2) % x_count, 0, 0)
    )
    return pl.pallas_call(
        mixed_body,
        grid_spec=pltpu.PrefetchScalarGridSpec(
            num_scalar_prefetch=1,
            grid=(local,),
            in_specs=[
                pl.BlockSpec((1, far_count, rows, width), lambda j, *_: (j, 0, 0, 0)),
                side,
                side,
                pl.BlockSpec((1, width, cols), lambda j, *_: (j, 0, 0)),
            ],
            out_specs=[VMEM_SPEC, VMEM_SPEC],
            scratch_shapes=[pltpu.VMEM((cols, cols), F32)],
        ),
        out_shape=[
            pltpu.VMEM((local * far_count, rows, cols), BF16),
            jax.ShapeDtypeStruct((local // 2, parent_rows, cols), F32),
        ],
        cost_estimate=pl.CostEstimate(
            flops=2 * local * far_count * rows * cols * width, bytes_accessed=8000000, transcendentals=0
        ),
        name="mixed_products",
    )(place, far_kernel, own, across, samples)


def coupling_body(base, slot_of, place, mixed, picked, mine, other, *_):
    x_count, blocks, out_rows, cols = mine.shape
    rows = mixed.shape[1]
    zero = jnp.zeros((rows, cols), BF16)
    core = place[0] % 2
    for b in range(0, blocks, 2):
        basis_rows = []
        for i in range(2):
            q = slot_of[base + b + i]
            start = pl.multiple_of((q % SLOTS) * rows, rows)
            basis_rows.append(picked[q // SLOTS, pl.ds(start, rows)])
        diagonal = jnp.concatenate(
            [
                jnp.concatenate([mixed[base + b], zero], axis=1),
                jnp.concatenate([zero, mixed[base + b + 1]], axis=1),
            ],
            axis=0,
        )
        both = lax.dot_general(
            jnp.concatenate(basis_rows, axis=0),
            diagonal,
            (((0,), (0,)), ((), ())),
            preferred_element_type=F32,
        )
        for i in range(2):
            part = both[:, i * cols : (i + 1) * cols].reshape(x_count, 2, out_rows, cols)
            for x in range(x_count):
                d = (x + x_count - place[0] // 2) % x_count
                mine[d, b + i] = jnp.where(core == 0, part[x, 0], part[x, 1]).astype(BF16)
                other[d, b + i] = jnp.where(core == 0, part[x, 1], part[x, 0]).astype(BF16)


def coupling_parts(half, slot_of, place, mixed, picked, x_count, local):
    blocks, rows, cols = mixed.shape
    shape = pltpu.VMEM((x_count, blocks // 2, cols // local, cols), BF16)
    again = [pltpu.VMEM(picked.shape, BF16)] if half == 0 else []
    return pl.pallas_call(
        functools.partial(coupling_body, half * blocks // 2),
        in_specs=[SMEM_SPEC, SMEM_SPEC, VMEM_SPEC, VMEM_SPEC],
        out_specs=[VMEM_SPEC] * (2 + len(again)),
        out_shape=[shape, shape] + again,
        input_output_aliases={3: 2} if again else {},
        cost_estimate=pl.CostEstimate(
            flops=2 * blocks * rows * cols * cols, bytes_accessed=4000000, transcendentals=0
        ),
        compiler_params=pltpu.CompilerParams(vmem_limit_bytes=12 << 20),
        name="coupling_parts_%d" % half,
    )(slot_of, place, in_vmem(mixed), in_vmem(picked))


def pair_body(mine, partner, kept, *sent):
    kept[...] = mine[0].astype(F32) + partner[0].astype(F32)
    for d, out in enumerate(sent):
        out[...] = (mine[d + 1].astype(F32) + partner[d + 1].astype(F32)).astype(BF16)


def pair_sums(half, mine, partner):
    shape = mine.shape[1:]
    return pl.pallas_call(
        pair_body,
        in_specs=[VMEM_SPEC] * 2,
        out_specs=[VMEM_SPEC] * mine.shape[0],
        out_shape=[pltpu.VMEM(shape, F32)] + [pltpu.VMEM(shape, BF16)] * (mine.shape[0] - 1),
        cost_estimate=pl.CostEstimate(flops=1000000, bytes_accessed=1000000, transcendentals=0),
        compiler_params=pltpu.CompilerParams(vmem_limit_bytes=8 << 20),
        name="pair_sums_%d" % half,
    )(in_vmem(mine), in_vmem(partner))


def finish_body(scale, *refs):
    total = refs[0][...]
    for moved in refs[1:4]:
        total = total + moved[...].astype(F32)
    refs[-1][...] = total * scale


def finish(half, scale, parts, result):
    blocks, rows, cols = parts[0].shape
    before = [] if result is None else [result]
    return pl.pallas_call(
        functools.partial(finish_body, scale),
        grid=(1,),
        in_specs=[VMEM_SPEC] * len(parts) + [HBM_SPEC] * len(before),
        out_specs=pl.BlockSpec(parts[0].shape, lambda i: (half, 0, 0)),
        out_shape=jax.ShapeDtypeStruct((2 * blocks, rows, cols), F32),
        input_output_aliases={len(parts): 0} if before else {},
        cost_estimate=pl.CostEstimate(flops=1000000, bytes_accessed=1000000, transcendentals=0),
        compiler_params=pltpu.CompilerParams(vmem_limit_bytes=8 << 20),
        name="finish_%d" % half,
    )(*[in_vmem(part) for part in parts], *before)


def per_device(far_kernel, near_kernel, samples, far_target):
    local, far_count, rows, width = far_kernel.shape
    cols = samples.shape[2]
    groups = lax.axis_size("y") * lax.axis_size("z")
    x_count = lax.axis_size("x")
    place = (lax.axis_index("x") * 2 + lax.axis_index("core")).astype(jnp.int32).reshape(1)

    def along_x(value, d):
        return lax.ppermute(value, "x", [(i, (i + d) % x_count) for i in range(x_count)])

    send, slot_of = far_products(far_kernel, samples, far_target, groups)
    received = lax.all_to_all(send, BLK, 0, 0, tiled=True)
    minus_near = near_products(near_kernel, samples)
    ids = received[:, SLOTS * rows :, 0].astype(jnp.int32)
    received = in_vmem(received)
    sketch = gather_sum(ids, received, minus_near)
    sketch = lax.all_to_all(sketch, ROW, 0, 0, tiled=True)
    rows_sent, basis = basis_of(sketch)
    basis_rows = lax.all_to_all(rows_sent, ROW, 0, 0, tiled=True)
    picked = lax.all_to_all(pick(ids, basis_rows), BLK, 0, 0, tiled=True)
    own = jnp.stack([basis] + [along_x(basis, d) for d in range(1, x_count)])
    own, basis_out = lax.optimization_barrier((own, basis_rows.astype(F32)))
    across = lax.ppermute(own, "core", [(0, 1), (1, 0)])
    mixed, parent = mixed_products(place, far_kernel, own, across, samples)
    coupling = None
    for part in range(2):
        mine, other, *again = coupling_parts(part, slot_of, place, mixed, picked, x_count, local)
        picked = again[0] if again else None
        partner = lax.ppermute(other, "core", [(0, 1), (1, 0)])
        kept, *sent = pair_sums(part, mine, partner)
        parts = [kept] + [along_x(sent[d - 1], d) for d in range(1, x_count)]
        coupling = finish(part, width**-0.5, parts, coupling)
    return basis_out, coupling.reshape(local, far_count, cols // local, cols), parent


def solution(mesh):
    fine = Mesh(mesh.devices.reshape(4, 8, 4, 2), ("y", "z", "x", "core"))
    return jax.shard_map(
        per_device,
        mesh=fine,
        in_specs=(
            P(BLK, None, ROW, None),
            P(BLK, None, ROW, None),
            P(BLK, None, None),
            P(BLK, None),
        ),
        out_specs=(P(BLK, ROW, None), P(BLK, None, ROW, None), P(BLK, ROW, None)),
        check_vma=False,
    )
```

```python
import functools

import jax
import jax.numpy as jnp
from jax import lax
from jax.experimental import pallas as pl
from jax.experimental.pallas import tpu as pltpu
from jax.sharding import Mesh, PartitionSpec as P

ITERS = 12
SLOTS = 4
META = 8
LIMIT = 61 << 20
BF16 = jnp.bfloat16
F32 = jnp.float32
SMEM_SPEC = pl.BlockSpec(memory_space=pltpu.SMEM)
VMEM_SPEC = pl.BlockSpec(memory_space=pltpu.VMEM)
HBM_SPEC = pl.BlockSpec(memory_space=pl.ANY)
BLK = ("y", "z")
ROW = ("x", "core")


def in_vmem(value):
    return pltpu.with_memory_space_constraint(value, pltpu.VMEM)


def far_body(y_count, first, *refs):
    if first:
        place, target, far, samples, *send, slot_of, group_slot, slot_id, buffer, count = refs
    else:
        slot_of, far, samples, *send, after, buffer = refs
    step = pl.program_id(0)
    pair, far_count, half, width = far.shape
    cols = buffer.shape[2]
    depth = buffer.shape[1]
    z_count = depth // (SLOTS * half)

    if first:

        @pl.when(step == 0)
        def _():
            for i in range(y_count * z_count):
                count[i] = 0
            for i in range(y_count * z_count * SLOTS):
                slot_id[i] = -1

    for i in range(pair):
        j = step * pair + i
        product = jnp.dot(far[i].reshape(far_count * half, width), samples[i], preferred_element_type=F32)
        product = product.astype(BF16).reshape(far_count, half, cols)
        for k in range(far_count):
            if first:
                local = target.shape[0]
                t = target[j, k]
                h = jnp.clip(t // local, 0, y_count * z_count - 1)
                g = (h // z_count + y_count - place[0]) % y_count * z_count + h % z_count
                c = jnp.minimum(count[g], SLOTS - 1)
                count[g] = c + 1
                q = g * SLOTS + c
                slot_of[j * far_count + k] = q
                group_slot[j * far_count + k] = h * SLOTS + c
                slot_id[q] = t % local
            else:
                q = slot_of[j * far_count + k]
            start = pl.multiple_of(q % (z_count * SLOTS) * half, half)
            buffer[q // (z_count * SLOTS), pl.ds(start, half)] = product[k]

    @pl.when(step == pl.num_programs(0) - 1)
    def _():
        if first:
            row = lax.broadcasted_iota(jnp.int32, (META, cols), 0)
            lane = lax.broadcasted_iota(jnp.int32, (META, cols), 1) // (cols // SLOTS)
        if not first:
            after[0] = slot_of[0]
        for d in range(y_count):
            send[d][:depth] = buffer[d]
            if first and d:
                ids = jnp.full(row.shape, -1, jnp.int32)
                for z in range(z_count):
                    for c in range(SLOTS):
                        value = slot_id[(d * z_count + z) * SLOTS + c]
                        ids = jnp.where((row == z) & (lane == c), value, ids)
                send[d][depth:] = ids.astype(F32).astype(BF16)


def far_products(part, far_kernel, samples, y_count, z_count, *scalars):
    local, far_count, rows, width = far_kernel.shape
    cols = samples.shape[2]
    half = rows // 2
    first = part == 0
    depth = z_count * SLOTS * half
    pair = 2
    blocks = local * far_count
    sends = [pltpu.VMEM((depth + (META if first and d else 0), cols), BF16) for d in range(y_count)]
    tables = [jax.ShapeDtypeStruct((1,), jnp.int32)]
    scratch = [pltpu.VMEM((y_count, depth, cols), BF16)]
    if first:
        tables = [jax.ShapeDtypeStruct((n,), jnp.int32) for n in (blocks, blocks, y_count * z_count * SLOTS)]
        scratch += [pltpu.SMEM((y_count * z_count,), jnp.int32)]
    return pl.pallas_call(
        functools.partial(far_body, y_count, first),
        grid=(local // pair,),
        in_specs=[SMEM_SPEC] * len(scalars)
        + [
            pl.BlockSpec((pair, far_count, half, width), lambda j: (j, 0, part, 0)),
            pl.BlockSpec((pair, width, cols), lambda j: (j, 0, 0)),
        ],
        out_specs=[VMEM_SPEC] * y_count + [SMEM_SPEC] * len(tables),
        out_shape=sends + tables,
        scratch_shapes=scratch,
        cost_estimate=pl.CostEstimate(
            flops=blocks * rows * width * cols, bytes_accessed=4000000, transcendentals=0
        ),
        compiler_params=pltpu.CompilerParams(vmem_limit_bytes=LIMIT),
    )(*scalars, far_kernel, samples)


def near_body(near, samples, minus_near):
    for i in range(2):
        near_sum = jnp.dot(near[i, 0], samples[i], preferred_element_type=F32)
        near_sum += jnp.dot(near[i, 1], samples[1 - i], preferred_element_type=F32)
        minus_near[i] = -near_sum


def near_products(near_kernel, samples):
    local, _, rows, width = near_kernel.shape
    cols = samples.shape[2]
    return pl.pallas_call(
        near_body,
        grid=(local // 2,),
        in_specs=[
            pl.BlockSpec((2, 2, rows, width), lambda j: (j, 0, 0, 0)),
            pl.BlockSpec((2, width, cols), lambda j: (j, 0, 0)),
        ],
        out_specs=pl.BlockSpec((2, rows, cols), lambda j: (j, 0, 0)),
        out_shape=jax.ShapeDtypeStruct((local, rows, cols), F32),
        cost_estimate=pl.CostEstimate(
            flops=4 * local * rows * width * cols, bytes_accessed=2500000, transcendentals=0
        ),
        name="near_products",
    )(near_kernel, samples)


def collect_body(whole_array, ids, place, *refs):
    *refs, acc0, acc1, acc2, acc3 = refs
    partial = (acc0, acc1, acc2, acc3)
    y_count, z_count, _ = ids.shape
    received, dense = refs[:y_count], refs[y_count:]
    local, half, cols = acc0.shape[0] - 1, acc0.shape[1], acc0.shape[2]
    row = lax.broadcasted_iota(jnp.int32, (META, cols), 0)
    lane = lax.broadcasted_iota(jnp.int32, (META, cols), 1) // (cols // SLOTS)
    for i in range(z_count):
        z = i if whole_array else (place[0] + i) % z_count
        for acc in partial:
            acc[...] = jnp.zeros_like(acc)
        for d, block in enumerate(received):
            for c in range(SLOTS):
                at = ids[d, z, c]
                at = jnp.where((at < 0) | (at >= local), local, at)
                start = pl.multiple_of((z * SLOTS + c) * half, half)
                partial[c][at] = partial[c][at] + block[pl.ds(start, half)].astype(F32)
        total = acc0[:local] + acc1[:local] + acc2[:local] + acc3[:local]
        total = total.reshape(local * half, cols).astype(BF16)
        if whole_array:
            dense[0][i, : local * half] = total
            table = jnp.full(row.shape, -1, jnp.int32)
            for d in range(y_count):
                for c in range(SLOTS):
                    table = jnp.where((row == d) & (lane == c), ids[d, z, c], table)
            dense[0][i, local * half :] = table.astype(F32).astype(BF16)
        else:
            dense[i][...] = total


def collect(part, ids, place, received, local, half):
    z_count = ids.shape[1]
    cols = received[0].shape[1]
    if part == 0:
        out = [jax.ShapeDtypeStruct((z_count, local * half + META, cols), BF16)]
    else:
        out = [pltpu.VMEM((local * half, cols), BF16)] * z_count
    return pl.pallas_call(
        functools.partial(collect_body, part == 0),
        in_specs=[SMEM_SPEC, SMEM_SPEC] + [VMEM_SPEC] * len(received),
        out_specs=[VMEM_SPEC] * len(out),
        out_shape=out,
        scratch_shapes=[pltpu.VMEM((local + 1, half, cols), F32)] * SLOTS,
        cost_estimate=pl.CostEstimate(flops=1000000, bytes_accessed=1600000, transcendentals=0),
        compiler_params=pltpu.CompilerParams(vmem_limit_bytes=LIMIT),
    )(ids, place, *[in_vmem(value) for value in received])


def dense_sum_body(first, *refs):
    *second, minus_near, sketch = refs
    local, rows, cols = sketch.shape
    half = rows // 2
    total = minus_near[:, :half]
    for z in range(first.shape[0]):
        total = total + first[z, : local * half].astype(F32).reshape(local, half, cols)
    sketch[:, :half] = total.astype(BF16)
    total = minus_near[:, half:]
    for value in second:
        total = total + value[...].astype(F32).reshape(local, half, cols)
    sketch[:, half:] = total.astype(BF16)


def dense_sum(first, second, minus_near):
    return pl.pallas_call(
        dense_sum_body,
        in_specs=[VMEM_SPEC] * (2 + len(second)),
        out_specs=VMEM_SPEC,
        out_shape=pltpu.VMEM(minus_near.shape, BF16),
        cost_estimate=pl.CostEstimate(flops=1000000, bytes_accessed=1500000, transcendentals=0),
        compiler_params=pltpu.CompilerParams(vmem_limit_bytes=LIMIT),
        name="dense_sum",
    )(in_vmem(first), *[in_vmem(value) for value in second], minus_near)


def split(value):
    high = value.astype(BF16)
    return high, (value - high.astype(F32)).astype(BF16)


def left(parts):
    return jnp.concatenate(parts, axis=1)


def right(parts):
    row = jnp.concatenate(parts, axis=1)
    return jnp.concatenate([row, row], axis=0)


def product(a, b):
    both = jnp.dot(a, b, preferred_element_type=F32)
    cols = both.shape[1] // 2
    return both[:, :cols] + both[:, cols:]


def basis_body(sketch, basis_rows, basis_half):
    full_width, cols = basis_half.shape
    values = sketch[...].reshape(full_width, cols)
    gram = lax.dot_general(values, values, (((0,), (0,)), ((), ())), preferred_element_type=F32)
    identity = (
        lax.broadcasted_iota(jnp.int32, (cols, cols), 0) == lax.broadcasted_iota(jnp.int32, (cols, cols), 1)
    ).astype(F32)
    trace = jnp.sum(jnp.sum(gram * identity, axis=1, keepdims=True), axis=0, keepdims=True)
    mean_sq = trace / (full_width * cols) + 1e-6
    level = gram / (full_width * cols * mean_sq)
    root = 1.5 * identity - 0.5 * level
    step_parts = root_parts = split(root)
    level_parts = split(level)
    for i in range(ITERS - 1):
        level = product(left(level_parts), right(step_parts))
        if i:
            root = product(left(step_parts), right(root_parts))
        level_parts, root_parts = split(level), split(root)
        step_parts = split(1.5 * identity - 0.5 * product(left(root_parts), right(level_parts)))
    root = product(left(step_parts), right(root_parts)) / jnp.sqrt(cols * mean_sq)
    result = product(values, jnp.concatenate(split(root), axis=1)).astype(BF16)
    basis_half[...] = result
    basis_rows[...] = result.reshape(basis_rows.shape)


def basis_of(sketch):
    local, rows, cols = sketch.shape
    return pl.pallas_call(
        basis_body,
        in_specs=[VMEM_SPEC],
        out_specs=[VMEM_SPEC] * 2,
        out_shape=[pltpu.VMEM(sketch.shape, BF16), jax.ShapeDtypeStruct((local * rows, cols), BF16)],
        cost_estimate=pl.CostEstimate(flops=500000000, bytes_accessed=1000000, transcendentals=0),
        name="basis_of",
    )(in_vmem(sketch))


def pick_body(ids, place, basis, send, sem):
    local, rows, _ = basis.shape
    z_count, y_count, _ = ids.shape

    def step(g, carry):
        for c in range(SLOTS):
            at = jnp.clip(ids[g % z_count, (place[0] + y_count - g // z_count) % y_count, c], 0, local - 1)
            pltpu.make_async_copy(basis.at[at], send.at[g, pl.ds(c * rows, rows)], sem).start()
        return carry

    lax.fori_loop(0, send.shape[0], step, 0, unroll=2)
    pltpu.make_async_copy(send, send, sem).wait()


def pick(ids, place, basis):
    _, rows, cols = basis.shape
    groups = ids.shape[0] * ids.shape[1]
    shape = (groups, SLOTS * rows, cols)
    return pl.pallas_call(
        pick_body,
        in_specs=[SMEM_SPEC, SMEM_SPEC, VMEM_SPEC],
        out_specs=HBM_SPEC,
        out_shape=jax.ShapeDtypeStruct(shape, BF16),
        scratch_shapes=[pltpu.SemaphoreType.DMA],
        cost_estimate=pl.CostEstimate(flops=1000000, bytes_accessed=3000000, transcendentals=0),
        name="pick",
    )(ids, place, in_vmem(basis))


def mixed_body(place, far, own, across, samples, mixed, parent, scratch):
    j = pl.program_id(0)
    far_count, rows, width = far.shape[1:]
    cols = own.shape[2]
    segment = jnp.where(j % 2 == place[0] % 2, own[0], across[0])
    values = jnp.dot(far[0].reshape(far_count * rows, width), segment, preferred_element_type=F32)
    mixed[pl.ds(j * far_count, far_count)] = values.astype(BF16).reshape(far_count, rows, cols)

    @pl.when(j % 2 == place[0] // 4)
    def _():
        scratch[...] = lax.dot_general(
            segment, samples[0], (((0,), (0,)), ((), ())), preferred_element_type=F32
        ) / jnp.sqrt(F32(width))
        count = parent.shape[1]
        start = pl.multiple_of((place[0] % 4) * count, count)
        parent[j // 2] = scratch[pl.ds(start, count)]


def mixed_products(place, far_kernel, own, across, samples):
    local, far_count, rows, width = far_kernel.shape
    x_count, _, cols = own.shape
    parent_rows = 2 * cols // local
    side = pl.BlockSpec(
        (1, width, cols), lambda j, place: ((place[0] // 2 + x_count - j // 2) % x_count, 0, 0)
    )
    return pl.pallas_call(
        mixed_body,
        grid_spec=pltpu.PrefetchScalarGridSpec(
            num_scalar_prefetch=1,
            grid=(local,),
            in_specs=[
                pl.BlockSpec((1, far_count, rows, width), lambda j, *_: (j, 0, 0, 0)),
                side,
                side,
                pl.BlockSpec((1, width, cols), lambda j, *_: (j, 0, 0)),
            ],
            out_specs=[VMEM_SPEC, VMEM_SPEC],
            scratch_shapes=[pltpu.VMEM((cols, cols), F32)],
        ),
        out_shape=[
            pltpu.VMEM((local * far_count, rows, cols), BF16),
            jax.ShapeDtypeStruct((local // 2, parent_rows, cols), F32),
        ],
        cost_estimate=pl.CostEstimate(
            flops=2 * local * far_count * rows * cols * width, bytes_accessed=8000000, transcendentals=0
        ),
        name="mixed_products",
    )(place, far_kernel, own, across, samples)


def coupling_body(base, slot_of, place, mixed, picked, mine, other, *_):
    x_count, blocks, out_rows, cols = mine.shape
    rows = mixed.shape[1]
    zero = jnp.zeros((rows, cols), BF16)
    core = place[0] % 2
    for b in range(0, blocks, 2):
        basis_rows = []
        for i in range(2):
            q = slot_of[base + b + i]
            start = pl.multiple_of((q % SLOTS) * rows, rows)
            basis_rows.append(picked[q // SLOTS, pl.ds(start, rows)])
        diagonal = jnp.concatenate(
            [
                jnp.concatenate([mixed[base + b], zero], axis=1),
                jnp.concatenate([zero, mixed[base + b + 1]], axis=1),
            ],
            axis=0,
        )
        both = lax.dot_general(
            jnp.concatenate(basis_rows, axis=0),
            diagonal,
            (((0,), (0,)), ((), ())),
            preferred_element_type=F32,
        )
        for i in range(2):
            part = both[:, i * cols : (i + 1) * cols].reshape(x_count, 2, out_rows, cols)
            for x in range(x_count):
                d = (x + x_count - place[0] // 2) % x_count
                mine[d, b + i] = jnp.where(core == 0, part[x, 0], part[x, 1]).astype(BF16)
                other[d, b + i] = jnp.where(core == 0, part[x, 1], part[x, 0]).astype(BF16)


def coupling_parts(half, slot_of, place, mixed, picked, x_count, local):
    blocks, rows, cols = mixed.shape
    shape = pltpu.VMEM((x_count, blocks // 2, cols // local, cols), BF16)
    again = [pltpu.VMEM(picked.shape, BF16)] if half == 0 else []
    return pl.pallas_call(
        functools.partial(coupling_body, half * blocks // 2),
        in_specs=[SMEM_SPEC, SMEM_SPEC, VMEM_SPEC, VMEM_SPEC],
        out_specs=[VMEM_SPEC] * (2 + len(again)),
        out_shape=[shape, shape] + again,
        input_output_aliases={3: 2} if again else {},
        cost_estimate=pl.CostEstimate(
            flops=2 * blocks * rows * cols * cols, bytes_accessed=4000000, transcendentals=0
        ),
        compiler_params=pltpu.CompilerParams(vmem_limit_bytes=12 << 20),
    )(slot_of, place, in_vmem(mixed), in_vmem(picked))


def pair_body(mine, partner, kept, *sent):
    kept[...] = mine[0].astype(F32) + partner[0].astype(F32)
    for d, out in enumerate(sent):
        out[...] = (mine[d + 1].astype(F32) + partner[d + 1].astype(F32)).astype(BF16)


def pair_sums(mine, partner):
    shape = mine.shape[1:]
    return pl.pallas_call(
        pair_body,
        in_specs=[VMEM_SPEC] * 2,
        out_specs=[VMEM_SPEC] * mine.shape[0],
        out_shape=[pltpu.VMEM(shape, F32)] + [pltpu.VMEM(shape, BF16)] * (mine.shape[0] - 1),
        cost_estimate=pl.CostEstimate(flops=1000000, bytes_accessed=1000000, transcendentals=0),
        compiler_params=pltpu.CompilerParams(vmem_limit_bytes=8 << 20),
    )(in_vmem(mine), in_vmem(partner))


def finish_body(scale, *refs):
    total = refs[0][...]
    for moved in refs[1:4]:
        total = total + moved[...].astype(F32)
    refs[-1][...] = total * scale


def finish(half, scale, parts, result):
    blocks, rows, cols = parts[0].shape
    before = [] if result is None else [result]
    return pl.pallas_call(
        functools.partial(finish_body, scale),
        grid=(1,),
        in_specs=[VMEM_SPEC] * len(parts) + [HBM_SPEC] * len(before),
        out_specs=pl.BlockSpec(parts[0].shape, lambda i: (half, 0, 0)),
        out_shape=jax.ShapeDtypeStruct((2 * blocks, rows, cols), F32),
        input_output_aliases={len(parts): 0} if before else {},
        cost_estimate=pl.CostEstimate(flops=1000000, bytes_accessed=1000000, transcendentals=0),
        compiler_params=pltpu.CompilerParams(vmem_limit_bytes=8 << 20),
    )(*[in_vmem(part) for part in parts], *before)


def per_device(far_kernel, near_kernel, samples, far_target):
    local, far_count, rows, width = far_kernel.shape
    cols = samples.shape[2]
    y_count, z_count = lax.axis_size("y"), lax.axis_size("z")
    half = rows // 2
    y_place, z_place = [lax.axis_index(name).astype(jnp.int32).reshape(1) for name in BLK]
    x_count = lax.axis_size("x")
    place = (lax.axis_index("x") * 2 + lax.axis_index("core")).astype(jnp.int32).reshape(1)

    def along_x(value, d):
        return lax.ppermute(value, "x", [(i, (i + d) % x_count) for i in range(x_count)])

    def shift(value, name, d, n):
        return lax.ppermute(value, name, [(i, (i + d) % n) for i in range(n)])

    *sent, slot_of, group_slot, slot_id = far_products(
        0, far_kernel, samples, y_count, z_count, y_place, far_target
    )
    moved = [shift(sent[d], "y", d, y_count) for d in range(1, y_count)]
    *later, after = far_products(1, far_kernel, samples, y_count, z_count, slot_of)
    later = [later[0]] + [shift(later[d], "y", d, y_count) for d in range(1, y_count)]
    minus_near = near_products(near_kernel, samples)
    slot_id, after, minus_near = lax.optimization_barrier((slot_id, after, minus_near))
    slot_id = jnp.where(after < 0, -1, slot_id)
    depth = z_count * SLOTS * half
    ids = jnp.stack([value[depth:, :: cols // SLOTS] for value in moved]).astype(jnp.int32)
    ids = jnp.concatenate([slot_id[: z_count * SLOTS].reshape(1, z_count, SLOTS), ids])
    (dense,) = collect(0, ids, z_place, [sent[0]] + moved, local, half)
    first = lax.all_to_all(dense, "z", 0, 0, tiled=True)
    dense = collect(1, ids, z_place, later, local, half)
    order = sorted(range(1, z_count), key=lambda d: -min(d, z_count - d))
    second = [dense[0]] + [shift(dense[d], "z", d, z_count) for d in order]
    ids = first[:, local * half : local * half + y_count, :: cols // SLOTS].astype(jnp.int32)
    sketch = dense_sum(first, second, minus_near)
    sketch = lax.all_to_all(sketch, ROW, 0, 0, tiled=True)
    rows_sent, basis = basis_of(sketch)
    basis_rows = lax.all_to_all(rows_sent, ROW, 0, 0, tiled=True)
    picked = lax.all_to_all(pick(ids, y_place, basis_rows), BLK, 0, 0, tiled=True)
    own = jnp.stack([basis] + [along_x(basis, d) for d in range(1, x_count)])
    own, basis_out = lax.optimization_barrier((own, basis_rows.astype(F32)))
    across = lax.ppermute(own, "core", [(0, 1), (1, 0)])
    mixed, parent = mixed_products(place, far_kernel, own, across, samples)
    coupling = None
    for part in range(2):
        mine, other, *again = coupling_parts(part, group_slot, place, mixed, picked, x_count, local)
        picked = again[0] if again else None
        partner = lax.ppermute(other, "core", [(0, 1), (1, 0)])
        kept, *sent = pair_sums(mine, partner)
        parts = [kept] + [along_x(sent[d - 1], d) for d in range(1, x_count)]
        coupling = finish(part, width**-0.5, parts, coupling)
    return basis_out, coupling.reshape(local, far_count, cols // local, cols), parent


def solution(mesh):
    fine = Mesh(mesh.devices.reshape(4, 8, 4, 2), ("y", "z", "x", "core"))
    return jax.shard_map(
        per_device,
        mesh=fine,
        in_specs=(
            P(BLK, None, ROW, None),
            P(BLK, None, ROW, None),
            P(BLK, None, None),
            P(BLK, None),
        ),
        out_specs=(P(BLK, ROW, None), P(BLK, None, ROW, None), P(BLK, ROW, None)),
        check_vma=False,
    )
```

```python
import functools

import jax
import jax.numpy as jnp
from jax import lax
from jax.experimental import pallas as pl
from jax.experimental.pallas import tpu as pltpu
from jax.sharding import Mesh, PartitionSpec as P

ITERS = 12
SLOTS = 4
META = 8
LIMIT = 61 << 20
ROOMY = 55 << 20
BF16 = jnp.bfloat16
F32 = jnp.float32
SMEM_SPEC = pl.BlockSpec(memory_space=pltpu.SMEM)
VMEM_SPEC = pl.BlockSpec(memory_space=pltpu.VMEM)
HBM_SPEC = pl.BlockSpec(memory_space=pl.ANY)
BLK = ("y", "z")
ROW = ("x", "core")


def in_vmem(value):
    return pltpu.with_memory_space_constraint(value, pltpu.VMEM)


def far_body(y_count, first, *refs):
    if first:
        place, target, far, samples, *send, slot_of, slot_id, buffer, count = refs
    else:
        slot_of, far, samples, *send, after, buffer = refs
    step = pl.program_id(0)
    pair, far_count, half, width = far.shape
    cols = buffer.shape[2]
    depth = buffer.shape[1]
    z_count = depth // (SLOTS * half)

    if first:

        @pl.when(step == 0)
        def _():
            for i in range(y_count * z_count):
                count[i] = 0
            for i in range(y_count * z_count * SLOTS):
                slot_id[i] = -1

    for i in range(pair):
        j = step * pair + i
        product = jnp.dot(far[i].reshape(far_count * half, width), samples[i], preferred_element_type=F32)
        product = product.astype(BF16).reshape(far_count, half, cols)
        for k in range(far_count):
            if first:
                local = target.shape[0]
                t = target[j, k]
                h = jnp.clip(t // local, 0, y_count * z_count - 1)
                g = (h // z_count + y_count - place[0]) % y_count * z_count + h % z_count
                c = jnp.minimum(count[g], SLOTS - 1)
                count[g] = c + 1
                q = g * SLOTS + c
                slot_of[j * far_count + k] = q
                slot_id[q] = t % local
            else:
                q = slot_of[j * far_count + k]
            start = pl.multiple_of(q % (z_count * SLOTS) * half, half)
            buffer[q // (z_count * SLOTS), pl.ds(start, half)] = product[k]

    @pl.when(step == pl.num_programs(0) - 1)
    def _():
        if first:
            row = lax.broadcasted_iota(jnp.int32, (META, cols), 0)
            lane = lax.broadcasted_iota(jnp.int32, (META, cols), 1) // (cols // SLOTS)
        if not first:
            after[0] = slot_of[0]
        for d in range(y_count):
            send[d][:depth] = buffer[d]
            if first and d:
                ids = jnp.full(row.shape, -1, jnp.int32)
                for z in range(z_count):
                    for c in range(SLOTS):
                        value = slot_id[(d * z_count + z) * SLOTS + c]
                        ids = jnp.where((row == z) & (lane == c), value, ids)
                send[d][depth:] = ids.astype(F32).astype(BF16)


def far_products(part, far_kernel, samples, y_count, z_count, *scalars):
    local, far_count, rows, width = far_kernel.shape
    cols = samples.shape[2]
    half = rows // 2
    first = part == 0
    depth = z_count * SLOTS * half
    pair = 2
    blocks = local * far_count
    sends = [pltpu.VMEM((depth + (META if first and d else 0), cols), BF16) for d in range(y_count)]
    tables = [jax.ShapeDtypeStruct((1,), jnp.int32)]
    scratch = [pltpu.VMEM((y_count, depth, cols), BF16)]
    if first:
        tables = [jax.ShapeDtypeStruct((n,), jnp.int32) for n in (blocks, y_count * z_count * SLOTS)]
        scratch += [pltpu.SMEM((y_count * z_count,), jnp.int32)]
    return pl.pallas_call(
        functools.partial(far_body, y_count, first),
        grid=(local // pair,),
        in_specs=[SMEM_SPEC] * len(scalars)
        + [
            pl.BlockSpec((pair, far_count, half, width), lambda j: (j, 0, part, 0)),
            pl.BlockSpec((pair, width, cols), lambda j: (j, 0, 0)),
        ],
        out_specs=[VMEM_SPEC] * y_count + [SMEM_SPEC] * len(tables),
        out_shape=sends + tables,
        scratch_shapes=scratch,
        cost_estimate=pl.CostEstimate(
            flops=blocks * rows * width * cols, bytes_accessed=4000000, transcendentals=0
        ),
        compiler_params=pltpu.CompilerParams(vmem_limit_bytes=LIMIT),
    )(*scalars, far_kernel, samples)


def near_body(near, samples, minus_near):
    for i in range(2):
        near_sum = jnp.dot(near[i, 0], samples[i], preferred_element_type=F32)
        near_sum += jnp.dot(near[i, 1], samples[1 - i], preferred_element_type=F32)
        minus_near[i] = -near_sum


def near_products(near_kernel, samples):
    local, _, rows, width = near_kernel.shape
    cols = samples.shape[2]
    return pl.pallas_call(
        near_body,
        grid=(local // 2,),
        in_specs=[
            pl.BlockSpec((2, 2, rows, width), lambda j: (j, 0, 0, 0)),
            pl.BlockSpec((2, width, cols), lambda j: (j, 0, 0)),
        ],
        out_specs=pl.BlockSpec((2, rows, cols), lambda j: (j, 0, 0)),
        out_shape=jax.ShapeDtypeStruct((local, rows, cols), F32),
        cost_estimate=pl.CostEstimate(
            flops=4 * local * rows * width * cols, bytes_accessed=2500000, transcendentals=0
        ),
        name="near_products",
    )(near_kernel, samples)


def collect_body(whole_array, ids, place, *refs):
    *refs, acc0, acc1, acc2, acc3 = refs
    partial = (acc0, acc1, acc2, acc3)
    y_count, z_count, _ = ids.shape
    received, dense = refs[:y_count], refs[y_count:]
    local, half, cols = acc0.shape[0] - 1, acc0.shape[1], acc0.shape[2]
    for i in range(z_count):
        z = i if whole_array else (place[0] + i) % z_count
        for acc in partial:
            acc[...] = jnp.zeros_like(acc)
        for d, block in enumerate(received):
            for c in range(SLOTS):
                at = ids[d, z, c]
                at = jnp.where((at < 0) | (at >= local), local, at)
                start = pl.multiple_of((z * SLOTS + c) * half, half)
                partial[c][at] = partial[c][at] + block[pl.ds(start, half)].astype(F32)
        total = acc0[:local] + acc1[:local] + acc2[:local] + acc3[:local]
        total = total.reshape(local * half, cols).astype(BF16)
        if whole_array:
            dense[0][i] = total
        else:
            dense[i][...] = total


def collect(part, ids, place, received, local, half):
    z_count = ids.shape[1]
    cols = received[0].shape[1]
    if part == 0:
        out = [jax.ShapeDtypeStruct((z_count, local * half, cols), BF16)]
    else:
        out = [pltpu.VMEM((local * half, cols), BF16)] * z_count
    return pl.pallas_call(
        functools.partial(collect_body, part == 0),
        in_specs=[SMEM_SPEC, SMEM_SPEC] + [VMEM_SPEC] * len(received),
        out_specs=[VMEM_SPEC] * len(out),
        out_shape=out,
        scratch_shapes=[pltpu.VMEM((local + 1, half, cols), F32)] * SLOTS,
        cost_estimate=pl.CostEstimate(flops=1000000, bytes_accessed=1600000, transcendentals=0),
        compiler_params=pltpu.CompilerParams(vmem_limit_bytes=LIMIT),
    )(ids, place, *[in_vmem(value) for value in received])


def dense_sum_body(first, *refs):
    *second, minus_near, sketch = refs
    local, rows, cols = sketch.shape
    half = rows // 2
    total = minus_near[:, :half]
    for z in range(first.shape[0]):
        total = total + first[z].astype(F32).reshape(local, half, cols)
    sketch[:, :half] = total.astype(BF16)
    total = minus_near[:, half:]
    for value in second:
        total = total + value[...].astype(F32).reshape(local, half, cols)
    sketch[:, half:] = total.astype(BF16)


def dense_sum(first, second, minus_near):
    return pl.pallas_call(
        dense_sum_body,
        in_specs=[VMEM_SPEC] * (2 + len(second)),
        out_specs=VMEM_SPEC,
        out_shape=pltpu.VMEM(minus_near.shape, BF16),
        cost_estimate=pl.CostEstimate(flops=1000000, bytes_accessed=1500000, transcendentals=0),
        compiler_params=pltpu.CompilerParams(vmem_limit_bytes=LIMIT),
        name="dense_sum",
    )(in_vmem(first), *[in_vmem(value) for value in second], minus_near)


def split(value):
    high = value.astype(BF16)
    return high, (value - high.astype(F32)).astype(BF16)


def left(parts):
    return jnp.concatenate(parts, axis=1)


def right(parts):
    row = jnp.concatenate(parts, axis=1)
    return jnp.concatenate([row, row], axis=0)


def product(a, b):
    both = jnp.dot(a, b, preferred_element_type=F32)
    cols = both.shape[1] // 2
    return both[:, :cols] + both[:, cols:]


def basis_body(sketch, basis_rows, basis_half):
    full_width, cols = basis_half.shape
    values = sketch[...].reshape(full_width, cols)
    gram = lax.dot_general(values, values, (((0,), (0,)), ((), ())), preferred_element_type=F32)
    identity = (
        lax.broadcasted_iota(jnp.int32, (cols, cols), 0) == lax.broadcasted_iota(jnp.int32, (cols, cols), 1)
    ).astype(F32)
    trace = jnp.sum(jnp.sum(gram * identity, axis=1, keepdims=True), axis=0, keepdims=True)
    mean_sq = trace / (full_width * cols) + 1e-6
    level = gram / (full_width * cols * mean_sq)
    root = 1.5 * identity - 0.5 * level
    step_parts = root_parts = split(root)
    level_parts = split(level)
    for i in range(ITERS - 1):
        level = product(left(level_parts), right(step_parts))
        if i:
            root = product(left(step_parts), right(root_parts))
        level_parts, root_parts = split(level), split(root)
        step_parts = split(1.5 * identity - 0.5 * product(left(root_parts), right(level_parts)))
    root = product(left(step_parts), right(root_parts)) / jnp.sqrt(cols * mean_sq)
    result = product(values, jnp.concatenate(split(root), axis=1)).astype(BF16)
    basis_half[...] = result
    basis_rows[...] = result.reshape(basis_rows.shape)


def basis_of(sketch):
    local, rows, cols = sketch.shape
    return pl.pallas_call(
        basis_body,
        in_specs=[VMEM_SPEC],
        out_specs=[VMEM_SPEC] * 2,
        out_shape=[pltpu.VMEM(sketch.shape, BF16), jax.ShapeDtypeStruct((local * rows, cols), BF16)],
        cost_estimate=pl.CostEstimate(flops=500000000, bytes_accessed=1000000, transcendentals=0),
        name="basis_of",
    )(in_vmem(sketch))


def spread_body(basis, first, second):
    local, rows, cols = basis.shape
    half = rows // 2
    values = basis[:, :half].reshape(local * half, cols)
    for z in range(first.shape[0]):
        first[z] = values
    second[...] = basis[:, half:].reshape(local * half, cols)


def spread(basis, z_count):
    local, rows, cols = basis.shape
    size = local * rows // 2
    return pl.pallas_call(
        spread_body,
        in_specs=[VMEM_SPEC],
        out_specs=[VMEM_SPEC] * 2,
        out_shape=[jax.ShapeDtypeStruct((z_count, size, cols), BF16), pltpu.VMEM((size, cols), BF16)],
        cost_estimate=pl.CostEstimate(flops=1000000, bytes_accessed=700000, transcendentals=0),
        name="spread",
    )(in_vmem(basis))


def pick_body(half, ids, place, *refs):
    y_count, z_count, _ = ids.shape
    bases, send = refs[:-y_count], refs[-y_count:]
    for i in range(z_count):
        z = i if len(bases) == 1 else (place[0] + z_count - i) % z_count
        source = bases[0].at[i] if len(bases) == 1 else bases[i]
        local = source.shape[0] // half
        for d, block in enumerate(send):
            for c in range(SLOTS):
                at = jnp.clip(ids[d, z, c], 0, local - 1)
                start = pl.multiple_of((z * SLOTS + c) * half, half)
                block[pl.ds(start, half)] = source[pl.ds(pl.multiple_of(at * half, half), half)]


def pick(ids, place, bases, half):
    y_count, z_count, _ = ids.shape
    cols = bases[0].shape[-1]
    return pl.pallas_call(
        functools.partial(pick_body, half),
        in_specs=[SMEM_SPEC, SMEM_SPEC] + [VMEM_SPEC] * len(bases),
        out_specs=[VMEM_SPEC] * y_count,
        out_shape=[pltpu.VMEM((z_count * SLOTS * half, cols), BF16)] * y_count,
        cost_estimate=pl.CostEstimate(flops=1000000, bytes_accessed=1600000, transcendentals=0),
        compiler_params=pltpu.CompilerParams(vmem_limit_bytes=ROOMY),
    )(ids, place, *[in_vmem(value) for value in bases])


def mixed_body(place, far, own, across, samples, mixed, parent, scratch):
    j = pl.program_id(0)
    far_count, rows, width = far.shape[1:]
    cols = own.shape[2]
    segment = jnp.where(j % 2 == place[0] % 2, own[0], across[0])
    values = jnp.dot(far[0].reshape(far_count * rows, width), segment, preferred_element_type=F32)
    mixed[pl.ds(j * far_count, far_count)] = values.astype(BF16).reshape(far_count, rows, cols)

    @pl.when(j % 2 == place[0] // 4)
    def _():
        scratch[...] = lax.dot_general(
            segment, samples[0], (((0,), (0,)), ((), ())), preferred_element_type=F32
        ) / jnp.sqrt(F32(width))
        count = parent.shape[1]
        start = pl.multiple_of((place[0] % 4) * count, count)
        parent[j // 2] = scratch[pl.ds(start, count)]


def mixed_products(place, far_kernel, own, across, samples):
    local, far_count, rows, width = far_kernel.shape
    x_count, _, cols = own.shape
    parent_rows = 2 * cols // local
    side = pl.BlockSpec(
        (1, width, cols), lambda j, place: ((place[0] // 2 + x_count - j // 2) % x_count, 0, 0)
    )
    return pl.pallas_call(
        mixed_body,
        grid_spec=pltpu.PrefetchScalarGridSpec(
            num_scalar_prefetch=1,
            grid=(local,),
            in_specs=[
                pl.BlockSpec((1, far_count, rows, width), lambda j, *_: (j, 0, 0, 0)),
                side,
                side,
                pl.BlockSpec((1, width, cols), lambda j, *_: (j, 0, 0)),
            ],
            out_specs=[VMEM_SPEC, VMEM_SPEC],
            scratch_shapes=[pltpu.VMEM((cols, cols), F32)],
        ),
        out_shape=[
            pltpu.VMEM((local * far_count, rows, cols), BF16),
            jax.ShapeDtypeStruct((local // 2, parent_rows, cols), F32),
        ],
        cost_estimate=pl.CostEstimate(
            flops=2 * local * far_count * rows * cols * width, bytes_accessed=8000000, transcendentals=0
        ),
        compiler_params=pltpu.CompilerParams(vmem_limit_bytes=ROOMY),
        name="mixed_products",
    )(place, far_kernel, own, across, samples)


def coupling_body(base, slot_of, place, mixed, *refs):
    if base:
        picked, mine, other = refs
    else:
        *received, mine, other, picked = refs
        y_count = picked.shape[1]
        for d in range(y_count):
            picked[0, d] = received[d][...]
            picked[1, d] = received[y_count + d][...]
    x_count, blocks, out_rows, cols = mine.shape
    rows = mixed.shape[1]
    half = rows // 2
    slots = picked.shape[2] // half
    zero = jnp.zeros((rows, cols), BF16)
    core = place[0] % 2
    for b in range(0, blocks, 2):
        basis_rows = []
        for i in range(2):
            q = slot_of[base + b + i]
            start = pl.multiple_of(q % slots * half, half)
            basis_rows += [picked[part, q // slots, pl.ds(start, half)] for part in range(2)]
        diagonal = jnp.concatenate(
            [
                jnp.concatenate([mixed[base + b], zero], axis=1),
                jnp.concatenate([zero, mixed[base + b + 1]], axis=1),
            ],
            axis=0,
        )
        both = lax.dot_general(
            jnp.concatenate(basis_rows, axis=0),
            diagonal,
            (((0,), (0,)), ((), ())),
            preferred_element_type=F32,
        )
        for i in range(2):
            part = both[:, i * cols : (i + 1) * cols].reshape(x_count, 2, out_rows, cols)
            for x in range(x_count):
                d = (x + x_count - place[0] // 2) % x_count
                mine[d, b + i] = jnp.where(core == 0, part[x, 0], part[x, 1]).astype(BF16)
                other[d, b + i] = jnp.where(core == 0, part[x, 1], part[x, 0]).astype(BF16)


def coupling_parts(part, slot_of, place, mixed, picked, x_count, local):
    blocks, rows, cols = mixed.shape
    shape = pltpu.VMEM((x_count, blocks // 2, cols // local, cols), BF16)
    again = [pltpu.VMEM((2, len(picked) // 2) + picked[0].shape, BF16)] if part == 0 else []
    return pl.pallas_call(
        functools.partial(coupling_body, part * blocks // 2),
        in_specs=[SMEM_SPEC, SMEM_SPEC] + [VMEM_SPEC] * (1 + len(picked)),
        out_specs=[VMEM_SPEC] * (2 + len(again)),
        out_shape=[shape, shape] + again,
        cost_estimate=pl.CostEstimate(
            flops=2 * blocks * rows * cols * cols, bytes_accessed=4000000, transcendentals=0
        ),
        compiler_params=pltpu.CompilerParams(vmem_limit_bytes=12 << 20),
    )(slot_of, place, in_vmem(mixed), *[in_vmem(value) for value in picked])


def pair_body(mine, partner, kept, *sent):
    kept[...] = mine[0].astype(F32) + partner[0].astype(F32)
    for d, out in enumerate(sent):
        out[...] = (mine[d + 1].astype(F32) + partner[d + 1].astype(F32)).astype(BF16)


def pair_sums(mine, partner):
    shape = mine.shape[1:]
    return pl.pallas_call(
        pair_body,
        in_specs=[VMEM_SPEC] * 2,
        out_specs=[VMEM_SPEC] * mine.shape[0],
        out_shape=[pltpu.VMEM(shape, F32)] + [pltpu.VMEM(shape, BF16)] * (mine.shape[0] - 1),
        cost_estimate=pl.CostEstimate(flops=1000000, bytes_accessed=1000000, transcendentals=0),
        compiler_params=pltpu.CompilerParams(vmem_limit_bytes=8 << 20),
    )(in_vmem(mine), in_vmem(partner))


def finish_body(scale, *refs):
    total = refs[0][...]
    for moved in refs[1:4]:
        total = total + moved[...].astype(F32)
    refs[-1][...] = total * scale


def finish(half, scale, parts, result):
    blocks, rows, cols = parts[0].shape
    before = [] if result is None else [result]
    return pl.pallas_call(
        functools.partial(finish_body, scale),
        grid=(1,),
        in_specs=[VMEM_SPEC] * len(parts) + [HBM_SPEC] * len(before),
        out_specs=pl.BlockSpec(parts[0].shape, lambda i: (half, 0, 0)),
        out_shape=jax.ShapeDtypeStruct((2 * blocks, rows, cols), F32),
        input_output_aliases={len(parts): 0} if before else {},
        cost_estimate=pl.CostEstimate(flops=1000000, bytes_accessed=1000000, transcendentals=0),
        compiler_params=pltpu.CompilerParams(vmem_limit_bytes=8 << 20),
    )(*[in_vmem(part) for part in parts], *before)


def per_device(far_kernel, near_kernel, samples, far_target):
    local, far_count, rows, width = far_kernel.shape
    cols = samples.shape[2]
    y_count, z_count = lax.axis_size("y"), lax.axis_size("z")
    half = rows // 2
    y_place, z_place = [lax.axis_index(name).astype(jnp.int32).reshape(1) for name in BLK]
    x_count = lax.axis_size("x")
    place = (lax.axis_index("x") * 2 + lax.axis_index("core")).astype(jnp.int32).reshape(1)

    def along_x(value, d):
        return lax.ppermute(value, "x", [(i, (i + d) % x_count) for i in range(x_count)])

    def shift(value, name, d, n):
        return lax.ppermute(value, name, [(i, (i + d) % n) for i in range(n)])

    *sent, slot_of, slot_id = far_products(
        0, far_kernel, samples, y_count, z_count, y_place, far_target
    )
    moved = [shift(sent[d], "y", d, y_count) for d in range(1, y_count)]
    *later, after = far_products(1, far_kernel, samples, y_count, z_count, slot_of)
    later = [later[0]] + [shift(later[d], "y", d, y_count) for d in range(1, y_count)]
    minus_near = near_products(near_kernel, samples)
    slot_id, after, minus_near = lax.optimization_barrier((slot_id, after, minus_near))
    slot_id = jnp.where(after < 0, -1, slot_id)
    depth = z_count * SLOTS * half
    ids = jnp.stack([value[depth:, :: cols // SLOTS] for value in moved]).astype(jnp.int32)
    ids = jnp.concatenate([slot_id[: z_count * SLOTS].reshape(1, z_count, SLOTS), ids])
    (dense,) = collect(0, ids, z_place, [sent[0]] + moved, local, half)
    first = lax.all_to_all(dense, "z", 0, 0, tiled=True)
    dense = collect(1, ids, z_place, later, local, half)
    order = sorted(range(1, z_count), key=lambda d: -min(d, z_count - d))
    second = [dense[0]] + [shift(dense[d], "z", d, z_count) for d in order]
    sketch = dense_sum(first, second, minus_near)
    sketch = lax.all_to_all(sketch, ROW, 0, 0, tiled=True)
    rows_sent, basis = basis_of(sketch)
    basis_rows = lax.all_to_all(rows_sent, ROW, 0, 0, tiled=True)
    first, second = spread(basis_rows, z_count)
    first = lax.all_to_all(first, "z", 0, 0, tiled=True)
    second = [second] + [shift(second, "z", d, z_count) for d in range(1, z_count)]
    chosen = pick(ids, z_place, [first], half)
    picked = [chosen[0]] + [shift(chosen[d], "y", -d, y_count) for d in range(1, y_count)]
    chosen = pick(ids, z_place, second, half)
    picked += [chosen[0]] + [shift(chosen[d], "y", -d, y_count) for d in range(1, y_count)]
    own = [along_x(basis, d) for d in range(1, x_count)]
    own = jnp.stack([basis] + own)
    own, basis_out = lax.optimization_barrier((own, basis_rows.astype(F32)))
    across = lax.ppermute(own, "core", [(0, 1), (1, 0)])
    mixed, parent = mixed_products(place, far_kernel, own, across, samples)
    coupling = None
    for part in range(2):
        mine, other, *again = coupling_parts(part, slot_of, place, mixed, picked, x_count, local)
        picked = again
        partner = lax.ppermute(other, "core", [(0, 1), (1, 0)])
        kept, *sent = pair_sums(mine, partner)
        parts = [kept] + [along_x(sent[d - 1], d) for d in range(1, x_count)]
        coupling = finish(part, width**-0.5, parts, coupling)
    return basis_out, coupling.reshape(local, far_count, cols // local, cols), parent


def solution(mesh):
    fine = Mesh(mesh.devices.reshape(4, 8, 4, 2), ("y", "z", "x", "core"))
    return jax.shard_map(
        per_device,
        mesh=fine,
        in_specs=(
            P(BLK, None, ROW, None),
            P(BLK, None, ROW, None),
            P(BLK, None, None),
            P(BLK, None),
        ),
        out_specs=(P(BLK, ROW, None), P(BLK, None, ROW, None), P(BLK, ROW, None)),
        check_vma=False,
    )
```

```python
import functools

import jax
import jax.numpy as jnp
from jax import lax
from jax.experimental import pallas as pl
from jax.experimental.pallas import tpu as pltpu
from jax.sharding import Mesh, PartitionSpec as P

ITERS = 12
SLOTS = 4
META = 8
LIMIT = 61 << 20
ROOMY = 55 << 20
BF16 = jnp.bfloat16
F32 = jnp.float32
SMEM_SPEC = pl.BlockSpec(memory_space=pltpu.SMEM)
VMEM_SPEC = pl.BlockSpec(memory_space=pltpu.VMEM)
HBM_SPEC = pl.BlockSpec(memory_space=pl.ANY)
BLK = ("y", "z")
ROW = ("x", "core")


def in_vmem(value):
    return pltpu.with_memory_space_constraint(value, pltpu.VMEM)


def far_body(y_count, first, *refs):
    if first:
        place, target, far, samples, *send, slot_of, slot_id, buffer, count = refs
    else:
        slot_of, far, samples, *send, after, buffer = refs
    step = pl.program_id(0)
    pair, far_count, half, width = far.shape
    cols = buffer.shape[2]
    depth = buffer.shape[1]
    z_count = depth // (SLOTS * half)

    if first:

        @pl.when(step == 0)
        def _():
            for i in range(y_count * z_count):
                count[i] = 0
            for i in range(y_count * z_count * SLOTS):
                slot_id[i] = -1

    for i in range(pair):
        j = step * pair + i
        product = jnp.dot(far[i].reshape(far_count * half, width), samples[i], preferred_element_type=F32)
        product = product.astype(BF16).reshape(far_count, half, cols)
        for k in range(far_count):
            if first:
                local = target.shape[0]
                t = target[j, k]
                h = jnp.clip(t // local, 0, y_count * z_count - 1)
                g = (h // z_count + y_count - place[0]) % y_count * z_count + h % z_count
                c = jnp.minimum(count[g], SLOTS - 1)
                count[g] = c + 1
                q = g * SLOTS + c
                slot_of[j * far_count + k] = q
                slot_id[q] = t % local
            else:
                q = slot_of[j * far_count + k]
            start = pl.multiple_of(q % (z_count * SLOTS) * half, half)
            buffer[q // (z_count * SLOTS), pl.ds(start, half)] = product[k]

    @pl.when(step == pl.num_programs(0) - 1)
    def _():
        if first:
            row = lax.broadcasted_iota(jnp.int32, (META, cols), 0)
            lane = lax.broadcasted_iota(jnp.int32, (META, cols), 1) // (cols // SLOTS)
        if not first:
            after[0] = slot_of[0]
        for d in range(y_count):
            send[d][:depth] = buffer[d]
            if first and d:
                ids = jnp.full(row.shape, -1, jnp.int32)
                for z in range(z_count):
                    for c in range(SLOTS):
                        value = slot_id[(d * z_count + z) * SLOTS + c]
                        ids = jnp.where((row == z) & (lane == c), value, ids)
                send[d][depth:] = ids.astype(F32).astype(BF16)


def far_products(part, far_kernel, samples, y_count, z_count, *scalars):
    local, far_count, rows, width = far_kernel.shape
    cols = samples.shape[2]
    half = rows // 2
    first = part == 0
    depth = z_count * SLOTS * half
    pair = 2
    blocks = local * far_count
    sends = [pltpu.VMEM((depth + (META if first and d else 0), cols), BF16) for d in range(y_count)]
    tables = [jax.ShapeDtypeStruct((1,), jnp.int32)]
    scratch = [pltpu.VMEM((y_count, depth, cols), BF16)]
    if first:
        tables = [jax.ShapeDtypeStruct((n,), jnp.int32) for n in (blocks, y_count * z_count * SLOTS)]
        scratch += [pltpu.SMEM((y_count * z_count,), jnp.int32)]
    return pl.pallas_call(
        functools.partial(far_body, y_count, first),
        grid=(local // pair,),
        in_specs=[SMEM_SPEC] * len(scalars)
        + [
            pl.BlockSpec((pair, far_count, half, width), lambda j: (j, 0, part, 0)),
            pl.BlockSpec((pair, width, cols), lambda j: (j, 0, 0)),
        ],
        out_specs=[VMEM_SPEC] * y_count + [SMEM_SPEC] * len(tables),
        out_shape=sends + tables,
        scratch_shapes=scratch,
        cost_estimate=pl.CostEstimate(
            flops=blocks * rows * width * cols, bytes_accessed=4000000, transcendentals=0
        ),
        compiler_params=pltpu.CompilerParams(vmem_limit_bytes=LIMIT),
    )(*scalars, far_kernel, samples)


def near_body(near, samples, minus_near):
    for i in range(2):
        near_sum = jnp.dot(near[i, 0], samples[i], preferred_element_type=F32)
        near_sum += jnp.dot(near[i, 1], samples[1 - i], preferred_element_type=F32)
        minus_near[i] = -near_sum


def near_products(near_kernel, samples):
    local, _, rows, width = near_kernel.shape
    cols = samples.shape[2]
    return pl.pallas_call(
        near_body,
        grid=(local // 2,),
        in_specs=[
            pl.BlockSpec((2, 2, rows, width), lambda j: (j, 0, 0, 0)),
            pl.BlockSpec((2, width, cols), lambda j: (j, 0, 0)),
        ],
        out_specs=pl.BlockSpec((2, rows, cols), lambda j: (j, 0, 0)),
        out_shape=jax.ShapeDtypeStruct((local, rows, cols), F32),
        cost_estimate=pl.CostEstimate(
            flops=4 * local * rows * width * cols, bytes_accessed=2500000, transcendentals=0
        ),
        name="near_products",
    )(near_kernel, samples)


def collect_body(whole_array, ids, place, *refs):
    *refs, acc0, acc1, acc2, acc3 = refs
    partial = (acc0, acc1, acc2, acc3)
    y_count, z_count, _ = ids.shape
    received, dense = refs[:y_count], refs[y_count:]
    local, half, cols = acc0.shape[0] - 1, acc0.shape[1], acc0.shape[2]
    for i in range(z_count):
        z = i if whole_array else (place[0] + i) % z_count
        for acc in partial:
            acc[...] = jnp.zeros_like(acc)
        for d, block in enumerate(received):
            for c in range(SLOTS):
                at = ids[d, z, c]
                at = jnp.where((at < 0) | (at >= local), local, at)
                start = pl.multiple_of((z * SLOTS + c) * half, half)
                partial[c][at] = partial[c][at] + block[pl.ds(start, half)].astype(F32)
        total = acc0[:local] + acc1[:local] + acc2[:local] + acc3[:local]
        total = total.reshape(local * half, cols).astype(BF16)
        if whole_array:
            dense[0][i] = total
        else:
            dense[i][...] = total


def collect(part, ids, place, received, local, half):
    z_count = ids.shape[1]
    cols = received[0].shape[1]
    if part == 0:
        out = [jax.ShapeDtypeStruct((z_count, local * half, cols), BF16)]
    else:
        out = [pltpu.VMEM((local * half, cols), BF16)] * z_count
    return pl.pallas_call(
        functools.partial(collect_body, part == 0),
        in_specs=[SMEM_SPEC, SMEM_SPEC] + [VMEM_SPEC] * len(received),
        out_specs=[VMEM_SPEC] * len(out),
        out_shape=out,
        scratch_shapes=[pltpu.VMEM((local + 1, half, cols), F32)] * SLOTS,
        cost_estimate=pl.CostEstimate(flops=1000000, bytes_accessed=1600000, transcendentals=0),
        compiler_params=pltpu.CompilerParams(vmem_limit_bytes=LIMIT),
    )(ids, place, *[in_vmem(value) for value in received])


def dense_sum_body(first, *refs):
    *second, minus_near, sketch = refs
    local, rows, cols = sketch.shape
    half = rows // 2
    total = minus_near[:, :half]
    for z in range(first.shape[0]):
        total = total + first[z].astype(F32).reshape(local, half, cols)
    sketch[:, :half] = total.astype(BF16)
    total = minus_near[:, half:]
    for value in second:
        total = total + value[...].astype(F32).reshape(local, half, cols)
    sketch[:, half:] = total.astype(BF16)


def dense_sum(first, second, minus_near):
    return pl.pallas_call(
        dense_sum_body,
        in_specs=[VMEM_SPEC] * (2 + len(second)),
        out_specs=VMEM_SPEC,
        out_shape=pltpu.VMEM(minus_near.shape, BF16),
        cost_estimate=pl.CostEstimate(flops=1000000, bytes_accessed=1500000, transcendentals=0),
        compiler_params=pltpu.CompilerParams(vmem_limit_bytes=LIMIT),
        name="dense_sum",
    )(in_vmem(first), *[in_vmem(value) for value in second], minus_near)


def split(value):
    high = value.astype(BF16)
    return high, (value - high.astype(F32)).astype(BF16)


def left(parts):
    return jnp.concatenate(parts, axis=1)


def right(parts):
    row = jnp.concatenate(parts, axis=1)
    return jnp.concatenate([row, row], axis=0)


def product(a, b):
    both = jnp.dot(a, b, preferred_element_type=F32)
    cols = both.shape[1] // 2
    return both[:, :cols] + both[:, cols:]


def basis_body(sketch, basis_rows, basis_half):
    full_width, cols = basis_half.shape
    values = sketch[...].reshape(full_width, cols)
    gram = lax.dot_general(values, values, (((0,), (0,)), ((), ())), preferred_element_type=F32)
    identity = (
        lax.broadcasted_iota(jnp.int32, (cols, cols), 0) == lax.broadcasted_iota(jnp.int32, (cols, cols), 1)
    ).astype(F32)
    trace = jnp.sum(jnp.sum(gram * identity, axis=1, keepdims=True), axis=0, keepdims=True)
    mean_sq = trace / (full_width * cols) + 1e-6
    level = gram / (full_width * cols * mean_sq)
    root = 1.5 * identity - 0.5 * level
    step_parts = root_parts = split(root)
    level_parts = split(level)
    for i in range(ITERS - 1):
        level = product(left(level_parts), right(step_parts))
        if i:
            root = product(left(step_parts), right(root_parts))
        level_parts, root_parts = split(level), split(root)
        step_parts = split(1.5 * identity - 0.5 * product(left(root_parts), right(level_parts)))
    root = product(left(step_parts), right(root_parts)) / jnp.sqrt(cols * mean_sq)
    result = product(values, jnp.concatenate(split(root), axis=1)).astype(BF16)
    basis_half[...] = result
    basis_rows[...] = result.reshape(basis_rows.shape)


def basis_of(sketch):
    local, rows, cols = sketch.shape
    return pl.pallas_call(
        basis_body,
        in_specs=[VMEM_SPEC],
        out_specs=[VMEM_SPEC] * 2,
        out_shape=[pltpu.VMEM(sketch.shape, BF16), jax.ShapeDtypeStruct((local * rows, cols), BF16)],
        cost_estimate=pl.CostEstimate(flops=500000000, bytes_accessed=1000000, transcendentals=0),
        name="basis_of",
    )(in_vmem(sketch))


def spread_body(basis, first, second):
    local, rows, cols = basis.shape
    half = rows // 2
    values = basis[:, :half].reshape(local * half, cols)
    for z in range(first.shape[0]):
        first[z] = values
    second[...] = basis[:, half:].reshape(local * half, cols)


def spread(basis, z_count):
    local, rows, cols = basis.shape
    size = local * rows // 2
    return pl.pallas_call(
        spread_body,
        in_specs=[VMEM_SPEC],
        out_specs=[VMEM_SPEC] * 2,
        out_shape=[jax.ShapeDtypeStruct((z_count, size, cols), BF16), pltpu.VMEM((size, cols), BF16)],
        cost_estimate=pl.CostEstimate(flops=1000000, bytes_accessed=700000, transcendentals=0),
        name="spread",
    )(in_vmem(basis))


def pick_body(half, ids, place, *refs):
    y_count, z_count, _ = ids.shape
    bases, send = refs[:-y_count], refs[-y_count:]
    for i in range(z_count):
        z = i if len(bases) == 1 else (place[0] + z_count - i) % z_count
        source = bases[0].at[i] if len(bases) == 1 else bases[i]
        local = source.shape[0] // half
        for d, block in enumerate(send):
            for c in range(SLOTS):
                at = jnp.clip(ids[d, z, c], 0, local - 1)
                start = pl.multiple_of((z * SLOTS + c) * half, half)
                block[pl.ds(start, half)] = source[pl.ds(pl.multiple_of(at * half, half), half)]


def pick(ids, place, bases, half):
    y_count, z_count, _ = ids.shape
    cols = bases[0].shape[-1]
    return pl.pallas_call(
        functools.partial(pick_body, half),
        in_specs=[SMEM_SPEC, SMEM_SPEC] + [VMEM_SPEC] * len(bases),
        out_specs=[VMEM_SPEC] * y_count,
        out_shape=[pltpu.VMEM((z_count * SLOTS * half, cols), BF16)] * y_count,
        cost_estimate=pl.CostEstimate(flops=1000000, bytes_accessed=1600000, transcendentals=0),
        compiler_params=pltpu.CompilerParams(vmem_limit_bytes=ROOMY),
    )(ids, place, *[in_vmem(value) for value in bases])


def mixed_body(place, far, own, across, samples, mixed, parent, scratch):
    step = pl.program_id(0)
    pair, far_count, rows, width = far.shape
    cols = own.shape[2]
    core, side = place[0] % 2, place[0] // 4
    segments = [jnp.where(core == i, own[0], across[0]) for i in range(pair)]
    for i in range(pair):
        values = jnp.dot(far[i].reshape(far_count * rows, width), segments[i], preferred_element_type=F32)
        start = pl.multiple_of((step * pair + i) * far_count, far_count)
        mixed[pl.ds(start, far_count)] = values.astype(BF16).reshape(far_count, rows, cols)
    scratch[...] = lax.dot_general(
        jnp.where(side == 0, segments[0], segments[1]),
        jnp.where(side == 0, samples[0], samples[1]),
        (((0,), (0,)), ((), ())),
        preferred_element_type=F32,
    ) / jnp.sqrt(F32(width))
    count = parent.shape[1]
    parent[step] = scratch[pl.ds(pl.multiple_of((place[0] % 4) * count, count), count)]


def mixed_products(place, far_kernel, own, across, samples):
    local, far_count, rows, width = far_kernel.shape
    x_count, _, cols = own.shape
    parent_rows = 2 * cols // local
    side = pl.BlockSpec(
        (1, width, cols), lambda j, place: ((place[0] // 2 + x_count - j) % x_count, 0, 0)
    )
    return pl.pallas_call(
        mixed_body,
        grid_spec=pltpu.PrefetchScalarGridSpec(
            num_scalar_prefetch=1,
            grid=(local // 2,),
            in_specs=[
                pl.BlockSpec((2, far_count, rows, width), lambda j, *_: (j, 0, 0, 0)),
                side,
                side,
                pl.BlockSpec((2, width, cols), lambda j, *_: (j, 0, 0)),
            ],
            out_specs=[VMEM_SPEC, VMEM_SPEC],
            scratch_shapes=[pltpu.VMEM((cols, cols), F32)],
        ),
        out_shape=[
            pltpu.VMEM((local * far_count, rows, cols), BF16),
            jax.ShapeDtypeStruct((local // 2, parent_rows, cols), F32),
        ],
        cost_estimate=pl.CostEstimate(
            flops=2 * local * far_count * rows * cols * width, bytes_accessed=8000000, transcendentals=0
        ),
        compiler_params=pltpu.CompilerParams(vmem_limit_bytes=ROOMY),
        name="mixed_products",
    )(place, far_kernel, own, across, samples)


def coupling_body(base, slot_of, place, mixed, *refs):
    if base:
        picked, mine, other = refs
    else:
        *received, mine, other, picked = refs
        y_count = picked.shape[1]
        for d in range(y_count):
            picked[0, d] = received[d][...]
            picked[1, d] = received[y_count + d][...]
    x_count, blocks, out_rows, cols = mine.shape
    rows = mixed.shape[1]
    half = rows // 2
    slots = picked.shape[2] // half
    zero = jnp.zeros((rows, cols), BF16)
    core = place[0] % 2
    for b in range(0, blocks, 2):
        basis_rows = []
        for i in range(2):
            q = slot_of[base + b + i]
            start = pl.multiple_of(q % slots * half, half)
            basis_rows += [picked[part, q // slots, pl.ds(start, half)] for part in range(2)]
        diagonal = jnp.concatenate(
            [
                jnp.concatenate([mixed[base + b], zero], axis=1),
                jnp.concatenate([zero, mixed[base + b + 1]], axis=1),
            ],
            axis=0,
        )
        both = lax.dot_general(
            jnp.concatenate(basis_rows, axis=0),
            diagonal,
            (((0,), (0,)), ((), ())),
            preferred_element_type=F32,
        )
        for i in range(2):
            part = both[:, i * cols : (i + 1) * cols].reshape(x_count, 2, out_rows, cols)
            for x in range(x_count):
                d = (x + x_count - place[0] // 2) % x_count
                mine[d, b + i] = jnp.where(core == 0, part[x, 0], part[x, 1]).astype(BF16)
                other[d, b + i] = jnp.where(core == 0, part[x, 1], part[x, 0]).astype(BF16)


def coupling_parts(part, slot_of, place, mixed, picked, x_count, local):
    blocks, rows, cols = mixed.shape
    shape = pltpu.VMEM((x_count, blocks // 2, cols // local, cols), BF16)
    again = [pltpu.VMEM((2, len(picked) // 2) + picked[0].shape, BF16)] if part == 0 else []
    return pl.pallas_call(
        functools.partial(coupling_body, part * blocks // 2),
        in_specs=[SMEM_SPEC, SMEM_SPEC] + [VMEM_SPEC] * (1 + len(picked)),
        out_specs=[VMEM_SPEC] * (2 + len(again)),
        out_shape=[shape, shape] + again,
        cost_estimate=pl.CostEstimate(
            flops=2 * blocks * rows * cols * cols, bytes_accessed=4000000, transcendentals=0
        ),
        compiler_params=pltpu.CompilerParams(vmem_limit_bytes=12 << 20),
    )(slot_of, place, in_vmem(mixed), *[in_vmem(value) for value in picked])


def pair_body(mine, partner, kept, *sent):
    kept[...] = mine[0].astype(F32) + partner[0].astype(F32)
    for d, out in enumerate(sent):
        out[...] = (mine[d + 1].astype(F32) + partner[d + 1].astype(F32)).astype(BF16)


def pair_sums(mine, partner):
    shape = mine.shape[1:]
    return pl.pallas_call(
        pair_body,
        in_specs=[VMEM_SPEC] * 2,
        out_specs=[VMEM_SPEC] * mine.shape[0],
        out_shape=[pltpu.VMEM(shape, F32)] + [pltpu.VMEM(shape, BF16)] * (mine.shape[0] - 1),
        cost_estimate=pl.CostEstimate(flops=1000000, bytes_accessed=1000000, transcendentals=0),
        compiler_params=pltpu.CompilerParams(vmem_limit_bytes=8 << 20),
    )(in_vmem(mine), in_vmem(partner))


def finish_body(scale, *refs):
    total = refs[0][...]
    for moved in refs[1:4]:
        total = total + moved[...].astype(F32)
    refs[-1][...] = total * scale


def finish(half, scale, parts, result):
    blocks, rows, cols = parts[0].shape
    before = [] if result is None else [result]
    return pl.pallas_call(
        functools.partial(finish_body, scale),
        grid=(1,),
        in_specs=[VMEM_SPEC] * len(parts) + [HBM_SPEC] * len(before),
        out_specs=pl.BlockSpec(parts[0].shape, lambda i: (half, 0, 0)),
        out_shape=jax.ShapeDtypeStruct((2 * blocks, rows, cols), F32),
        input_output_aliases={len(parts): 0} if before else {},
        cost_estimate=pl.CostEstimate(flops=1000000, bytes_accessed=1000000, transcendentals=0),
        compiler_params=pltpu.CompilerParams(vmem_limit_bytes=8 << 20),
    )(*[in_vmem(part) for part in parts], *before)


def per_device(far_kernel, near_kernel, samples, far_target):
    local, far_count, rows, width = far_kernel.shape
    cols = samples.shape[2]
    y_count, z_count = lax.axis_size("y"), lax.axis_size("z")
    half = rows // 2
    y_place, z_place = [lax.axis_index(name).astype(jnp.int32).reshape(1) for name in BLK]
    x_count = lax.axis_size("x")
    place = (lax.axis_index("x") * 2 + lax.axis_index("core")).astype(jnp.int32).reshape(1)

    def along_x(value, d):
        return lax.ppermute(value, "x", [(i, (i + d) % x_count) for i in range(x_count)])

    def shift(value, name, d, n):
        return lax.ppermute(value, name, [(i, (i + d) % n) for i in range(n)])

    *sent, slot_of, slot_id = far_products(
        0, far_kernel, samples, y_count, z_count, y_place, far_target
    )
    moved = [shift(sent[d], "y", d, y_count) for d in range(1, y_count)]
    *later, after = far_products(1, far_kernel, samples, y_count, z_count, slot_of)
    later = [later[0]] + [shift(later[d], "y", d, y_count) for d in range(1, y_count)]
    minus_near = near_products(near_kernel, samples)
    slot_id, after, minus_near = lax.optimization_barrier((slot_id, after, minus_near))
    slot_id = jnp.where(after < 0, -1, slot_id)
    depth = z_count * SLOTS * half
    ids = jnp.stack([value[depth:, :: cols // SLOTS] for value in moved]).astype(jnp.int32)
    ids = jnp.concatenate([slot_id[: z_count * SLOTS].reshape(1, z_count, SLOTS), ids])
    (dense,) = collect(0, ids, z_place, [sent[0]] + moved, local, half)
    first = lax.all_to_all(dense, "z", 0, 0, tiled=True)
    dense = collect(1, ids, z_place, later, local, half)
    order = sorted(range(1, z_count), key=lambda d: -min(d, z_count - d))
    second = [dense[0]] + [shift(dense[d], "z", d, z_count) for d in order]
    sketch = dense_sum(first, second, minus_near)
    sketch = lax.all_to_all(sketch, ROW, 0, 0, tiled=True)
    rows_sent, basis = basis_of(sketch)
    basis_rows = lax.all_to_all(rows_sent, ROW, 0, 0, tiled=True)
    first, second = spread(basis_rows, z_count)
    first = lax.all_to_all(first, "z", 0, 0, tiled=True)
    second = [second] + [shift(second, "z", d, z_count) for d in range(1, z_count)]
    chosen = pick(ids, z_place, [first], half)
    picked = [chosen[0]] + [shift(chosen[d], "y", -d, y_count) for d in range(1, y_count)]
    chosen = pick(ids, z_place, second, half)
    picked += [chosen[0]] + [shift(chosen[d], "y", -d, y_count) for d in range(1, y_count)]
    own = [along_x(basis, d) for d in range(1, x_count)]
    own = jnp.stack([basis] + own)
    own, basis_out = lax.optimization_barrier((own, basis_rows.astype(F32)))
    across = lax.ppermute(own, "core", [(0, 1), (1, 0)])
    mixed, parent = mixed_products(place, far_kernel, own, across, samples)
    coupling = None
    for part in range(2):
        mine, other, *again = coupling_parts(part, slot_of, place, mixed, picked, x_count, local)
        picked = again
        partner = lax.ppermute(other, "core", [(0, 1), (1, 0)])
        kept, *sent = pair_sums(mine, partner)
        parts = [kept] + [along_x(sent[d - 1], d) for d in range(1, x_count)]
        coupling = finish(part, width**-0.5, parts, coupling)
    return basis_out, coupling.reshape(local, far_count, cols // local, cols), parent


def solution(mesh):
    fine = Mesh(mesh.devices.reshape(4, 8, 4, 2), ("y", "z", "x", "core"))
    return jax.shard_map(
        per_device,
        mesh=fine,
        in_specs=(
            P(BLK, None, ROW, None),
            P(BLK, None, ROW, None),
            P(BLK, None, None),
            P(BLK, None),
        ),
        out_specs=(P(BLK, ROW, None), P(BLK, None, ROW, None), P(BLK, ROW, None)),
        check_vma=False,
    )
```
